32 devices in a mesh: req: 8 (over z, x), head: 4 (over y, core).
Axes of the slice: x: 2, y: 2, z: 4, core: 2. Of those that a mesh axis runs over, the one named last changes fastest.
Arguments:
- hidden_state: bfloat16 [64, 2048], P('req'), may hold values from -6 to 6
- attend_gain: float32 [2048], replicated, may hold values from 0.1 to 1.9
- input_weight: bfloat16 [2048, 3, 2048], P(None, None, 'head'), may hold values from -0.125 to 0.125
- input_bias: float32 [3, 2048], P(None, 'head'), may hold values from -3 to 3
- output_weight: bfloat16 [2048, 2048], P('head'), may hold values from -0.125 to 0.125
- window_cache: bfloat16 [64, 2, 2048, 2048], P('req', None, None, 'head'), may hold values from -9 to 9
- sink_cache: bfloat16 [64, 2, 4, 2048], P('req', None, None, 'head'), may hold values from -3000 to 3000
- lengths: int32 [64], P('req'), may hold values from 16 to 32768, as said below
- expert_index: int32 [64, 4], P('req'), may hold values from 0 to 31, all different within a row; in each aligned block of 8 rows (0 to 7, 8 to 15, ...) at most 2 rows name the same one
- router_weight: float32 [64, 4], P('req'), may hold values from 0.05 to 0.5
- mixture_gain: float32 [2048], replicated, may hold values from 0.1 to 1.9
- expert_gate_up: bfloat16 [2, 45056, 2048], P(None, ('req', 'head')), may hold values from -0.125 to 0.125
- expert_down: bfloat16 [45056, 2048], P(('req', 'head')), may hold values from -0.3125 to 0.3125
- shared_gate_up: bfloat16 [2, 2048, 5632], P(None, 'req', 'head'), may hold values from -0.125 to 0.125
- shared_down: bfloat16 [5632, 2048], P('head', 'req'), may hold values from -0.078125 to 0.078125
- shared_gate: float32 [2048], replicated, may hold values from -0.125 to 0.125
Outputs:
- layer_out: bfloat16 [64, 2048], P('req', 'head')
- new_kv: bfloat16 [64, 2, 2048], P('req', None, 'head')
The draws below stay inside these ranges and needn't reach their ends.
Inputs may be any that keep to these rules, and one draw needn't show every extreme that they name: Request r has lengths[r] cached tokens and its new token takes position lengths[r]; some request has exactly 32768 cached tokens and some has 16. `expert_index`: each row names 4 different experts; within the rows of one index of req (aligned blocks of 8 rows) no expert is named more than 2 times, a bound that some block reaches.
All inputs are finite; a program needn't handle non-finite values.
Results may differ from the reference program's by a relative error of at most 0.014.
The reference program's roundings to bfloat16 on the way count: a program that leaves them out, or rounds other values in their place, can miss the bound.
Values may be sent and summed in bfloat16 or wider, within the bound.
No kernel may reach another device: no remote copies, remote signals or barrier semaphores. Data moves between devices by JAX's collectives and lax.ppermute only.
A program may use at most 256 MiB of HBM per device.

```python
import math
import jax
import jax.numpy as jnp
import numpy as np
from jax import lax

D = 2048
HEADS = 16
HD = 128
EXPERTS = 32
FE = 1408
TOP = 4
FS = 5632
SINKS = 4
WINDOW = 2048
MAXLEN = 32768
CAP = 2
REQ_DEV = 8
REQ = 64


def draw_sink_cache(key, part):
    key_one = jax.random.fold_in(key, 0)
    base_values = 1.5 * jax.random.normal(key_one, (REQ, 2, SINKS, HEADS * HD), jnp.float32)
    return base_values.astype(jnp.bfloat16)


def draw_lengths(key, part):
    key_one, key_two, key_three, key_four = jax.random.split(key, 4)
    shorter = jax.random.randint(key_one, (REQ,), 16, SINKS + WINDOW)
    longer = jax.random.randint(key_two, (REQ,), SINKS + WINDOW, MAXLEN + 1)
    picking = jax.random.randint(key_three, (REQ,), 0, 2)
    values = jnp.where(picking == 1, longer, shorter)
    ordering = jax.random.permutation(key_four, REQ)
    values = values.at[ordering[0]].set(MAXLEN)
    values = values.at[ordering[1]].set(16)
    return values.astype(jnp.int32)


def strengthened(result, rng, source, target, blocks, factor):
    owner, partner = [(jnp.arange(result.shape[position]) // (result.shape[position] // blocks)).reshape([-1 if axis == position else 1 for axis in range(result.ndim)]) for position in (source, target)]
    chosen = jax.random.permutation(rng, blocks)[partner]
    strong = (owner == chosen) | (owner == (partner + blocks // 2) % blocks)
    return jnp.where(strong, factor * result, result)


def shard_levels(stream_key, shape, shards, least, top_value):
    level = 1.0
    for position, blocks in shards:
        steps = jax.random.uniform(jax.random.fold_in(jax.random.fold_in(stream_key, 6), position), (blocks,), jnp.float32, least / len(shards), top_value / len(shards))
        level = level * jnp.repeat(jnp.exp(steps), shape[position] // blocks).reshape((-1,) + (1,) * (len(shape) - 1 - position))
    return level


def shared_out(key, own, number, rows, amount, top, bound, slope):
    sequence = jax.random.permutation(key, amount)
    heavy_load, ordinary = portions_of(amount, rows * top, bound, slope, True), portions_of(amount, rows * top, bound, slope, False)
    places = jnp.arange(amount)

    def named(tallies, offset_by):
        used = int((tallies > 0).sum())
        fixed = max(1, used // 4)
        moved = fixed + (places - fixed + offset_by * (used - fixed)) % max(1, amount - fixed)
        return jnp.zeros((amount,), jnp.int32).at[sequence[jnp.where(places < fixed, places, moved)]].set(jnp.asarray(tallies, jnp.int32))

    tallies = jnp.where(number % 4 == 0, named(heavy_load, number // 4), named(ordinary, number - number // 4 - 1))
    mixed = jax.random.permutation(jax.random.fold_in(own, 3), amount)
    giver, taker = mixed[0:amount // 2 * 2:2], mixed[1:amount // 2 * 2:2]
    room = jnp.minimum(tallies[giver] - 1, bound - tallies[taker]) // 2
    room = jnp.where((giver == sequence[0]) | (taker == sequence[0]) | (tallies[taker] == 0), 0, jnp.maximum(room, 0))
    moved = jax.random.randint(jax.random.fold_in(own, 4), (amount // 2,), 0, 1 << 20) % (room + 1)
    tallies = tallies.at[giver].add(-moved).at[taker].add(moved)
    labels = jnp.searchsorted(jnp.cumsum(tallies), jnp.arange(rows * top), side="right").astype(jnp.int32)
    grid = labels.reshape(top, rows).T
    grid = grid[jax.random.permutation(jax.random.fold_in(own, 1), rows)]
    offset_by = jax.random.randint(jax.random.fold_in(own, 2), (rows, 1), 0, top)
    return jnp.take_along_axis(grid, (jnp.arange(top)[None, :] + offset_by) % top, axis=1)


def portions_of(amount, total, limit, slope, full):
    portions = [(1 << 20) // math.isqrt(grade ** slope) + 1 for grade in range(1, amount + 1)]
    largest = limit if full else min(limit, max(-(-total // amount), total * portions[0] // sum(portions)))
    least = 1 if total - largest >= amount - 1 else 0
    given, rest = [largest] + [least] * (amount - 1), total - largest - least * (amount - 1)
    while rest > 0:
        free = [i for i in range(1, amount) if given[i] < largest] or [i for i in range(1, amount) if given[i] < limit]
        pool, remaining = sum([portions[i] for i in free]), rest
        for i in free:
            extra = min(limit - given[i], max(1, remaining * portions[i] // pool), rest)
            given[i] = given[i] + extra
            rest = rest - extra
    return np.array(given)


def centred(rng, dims, width, reach, cuts=(), held_as=jnp.bfloat16):
    values = jax.random.normal(rng, dims, jnp.float32) * width
    if len(cuts) > 0:
        values = shard_levels(rng, dims, cuts, -0.22, 0.18) * values
    return jnp.clip(values, min=-reach, max=reach).astype(held_as)


def heavy_noise(key, dims, scale, limit, cuts, heavy, held_as=jnp.bfloat16):
    drawn = scale * jax.random.normal(key, dims, jnp.float32)
    if cuts:
        drawn = drawn * shard_levels(key, dims, cuts, -0.22, 0.18)
    return jnp.clip(strengthened(drawn, jax.random.fold_in(key, 3), *heavy), -limit, limit).astype(held_as)


def setup_inputs(seed: int = 0) -> dict:
    key_of = jax.random.split(jax.random.key(seed), 17)
    hidden_state = centred(key_of[0], (REQ, D), 1.0, 6.0, ((0, 8),))
    attend_gain = jnp.clip(1.0 + 0.18 * jax.random.normal(key_of[1], (D,), jnp.float32), 0.1, 1.9)
    input_weight = centred(key_of[2], (D, 3, HEADS * HD), D ** -0.5, 0.125, ((2, 4),))
    input_bias = centred(key_of[3], (3, HEADS * HD), 0.5, 3.0, ((1, 4),), jnp.float32)
    output_weight = centred(key_of[4], (HEADS * HD, D), (HEADS * HD) ** -0.5, 0.125, ((0, 4),))
    window_cache = centred(key_of[5], (REQ, 2, WINDOW, HEADS * HD), 1.5, 9.0, ((0, 8), (3, 4)))
    sink_cache = draw_sink_cache(jax.random.fold_in(key_of[16], 71), 0)
    lengths = draw_lengths(jax.random.fold_in(key_of[16], 71), 0)
    expert_index_keys = jax.random.split(jax.random.fold_in(key_of[8], 1), REQ // REQ_DEV)
    expert_index_turns = jax.random.permutation(jax.random.fold_in(key_of[8], 3), REQ // REQ_DEV)
    expert_index = jax.vmap(lambda own, number: shared_out(jax.random.fold_in(key_of[8], 2), own, number, REQ_DEV, EXPERTS, TOP, CAP, 2))(expert_index_keys, expert_index_turns).reshape((REQ, TOP))
    router_weight = jnp.clip(0.05 + 0.45 * jax.random.uniform(key_of[9], (REQ, TOP), jnp.float32) ** shard_levels(key_of[9], (REQ, TOP), ((0, 8),), -0.2, 0.2), 0.05, 0.5)
    mixture_gain = jnp.clip(1.0 + 0.18 * jax.random.normal(key_of[10], (D,), jnp.float32), 0.1, 1.9)
    expert_gate_up = centred(key_of[11], (2, EXPERTS * FE, D), D ** -0.5, 0.125, ((1, 32),))
    expert_down = heavy_noise(key_of[12], (EXPERTS * FE, D), FE ** -0.5, 0.3125, ((0, 32),), (0, 1, 32, 2.75))
    shared_gate_up = centred(key_of[13], (2, D, FS), D ** -0.5, 0.125, ((1, 8), (2, 4)))
    shared_down = centred(key_of[14], (FS, D), FS ** -0.5, 0.078125, ((0, 4), (1, 8)))
    shared_gate = centred(key_of[15], (D,), D ** -0.5, 0.125, (), jnp.float32)
    return dict(hidden_state=hidden_state, attend_gain=attend_gain, input_weight=input_weight, input_bias=input_bias, output_weight=output_weight, window_cache=window_cache, sink_cache=sink_cache, lengths=lengths, expert_index=expert_index, router_weight=router_weight, mixture_gain=mixture_gain, expert_gate_up=expert_gate_up, expert_down=expert_down, shared_gate_up=shared_gate_up, shared_down=shared_down, shared_gate=shared_gate)


EPSILON = 1e-06
ROPE_BASE = 1000000.0

def rms_scale(values, gains):
    mean_square = lax.optimization_barrier(jnp.mean(values * values, axis=-1, keepdims=True))
    return values * lax.rsqrt(mean_square + EPSILON) * gains

def rotate(vectors, positions):
    half_depth = vectors.shape[-1] // 2
    steps_half = jnp.arange(half_depth).astype(jnp.float32)
    frequencies = jnp.float32(ROPE_BASE) ** (-(2.0 / vectors.shape[-1]) * steps_half)
    angles = positions.astype(jnp.float32)[:, None] * frequencies[None, :]
    cosine = jnp.cos(angles)[:, None, :]
    sine_terms = jnp.sin(angles)[:, None, :]
    lower_half = vectors[..., :half_depth]
    upper_half = vectors[..., half_depth:]
    return jnp.concatenate([lower_half * cosine - upper_half * sine_terms, upper_half * cosine + lower_half * sine_terms], axis=-1)

def reference(hidden_state, attend_gain, input_weight, input_bias, output_weight, window_cache, sink_cache, lengths, expert_index, router_weight, mixture_gain, expert_gate_up, expert_down, shared_gate_up, shared_down, shared_gate):
    head_width = HEADS * HD
    normed = rms_scale(hidden_state.astype(jnp.float32), attend_gain).astype(jnp.bfloat16)
    projected = jnp.dot(normed, input_weight.reshape(D, 3 * head_width), preferred_element_type=jnp.float32) + input_bias.reshape(3 * head_width)
    projected = projected.reshape(REQ, 3, HEADS, HD)
    queries = rotate(projected[:, 0], lengths).astype(jnp.bfloat16)
    fresh_key = rotate(projected[:, 1], lengths).astype(jnp.bfloat16)
    fresh_value = projected[:, 2].astype(jnp.bfloat16)
    new_kv = jnp.stack([fresh_key.reshape(REQ, head_width), fresh_value.reshape(REQ, head_width)], axis=1)

    def attend_one(pieces):
        query_one, fresh_pair, window_one, sinks_one, length_one = pieces
        fresh_slot = ((length_one - SINKS) % WINDOW).astype(jnp.int32)
        window_one = lax.dynamic_update_slice(window_one, fresh_pair[:, None, :], (jnp.int32(0), fresh_slot, jnp.int32(0)))
        live_count = jnp.minimum(length_one - SINKS + 1, WINDOW)
        key_rows = jnp.concatenate([sinks_one[0], window_one[0]], axis=0).reshape(SINKS + WINDOW, HEADS, HD).astype(jnp.float32)
        value_rows = jnp.concatenate([sinks_one[1], window_one[1]], axis=0).reshape(SINKS + WINDOW, HEADS, HD).astype(jnp.float32)
        scores = jnp.einsum('hd,shd->hs', query_one.astype(jnp.float32), key_rows) / math.sqrt(HD)
        positions = jnp.arange(SINKS + WINDOW)
        keeping = (positions < SINKS) | (positions - SINKS < live_count)
        scores = jnp.where(keeping[None, :], scores, -jnp.inf)
        weights = jax.nn.softmax(scores, axis=-1).astype(jnp.bfloat16)
        return jnp.einsum('hs,shd->hd', weights.astype(jnp.float32), value_rows).astype(jnp.bfloat16)
    attended = lax.map(attend_one, (queries, new_kv, window_cache, sink_cache, lengths))
    resid = hidden_state.astype(jnp.float32) + jnp.dot(attended.reshape(REQ, head_width), output_weight, preferred_element_type=jnp.float32)
    tokens = rms_scale(resid, mixture_gain).astype(jnp.bfloat16)
    expert_hot = (expert_index[:, :, None] == jnp.arange(EXPERTS)[None, None, :]).astype(jnp.float32)
    combine = lax.optimization_barrier(jnp.sum(expert_hot * router_weight[:, :, None], axis=1))
    gate_up_all = expert_gate_up.reshape(2, EXPERTS, FE, D)
    down_all = expert_down.reshape(EXPERTS, FE, D)

    def expert_step(running, pieces):
        gate_rows, up_rows, down_rows, weight_col = pieces
        gate_terms = jnp.dot(tokens, gate_rows.T, preferred_element_type=jnp.float32)
        up_terms = jnp.dot(tokens, up_rows.T, preferred_element_type=jnp.float32)
        hidden_units = (jax.nn.silu(gate_terms) * up_terms).astype(jnp.bfloat16)
        return (running + weight_col[:, None] * jnp.dot(hidden_units, down_rows, preferred_element_type=jnp.float32), None)
    routed, _ = lax.scan(expert_step, jnp.zeros((REQ, D), jnp.float32), (gate_up_all[0], gate_up_all[1], down_all, combine.T))
    gate_value = jax.nn.sigmoid(jnp.dot(tokens.astype(jnp.float32), shared_gate, precision=lax.Precision.HIGHEST))
    shared_gates = jnp.dot(tokens, shared_gate_up[0], preferred_element_type=jnp.float32)
    shared_ups = jnp.dot(tokens, shared_gate_up[1], preferred_element_type=jnp.float32)
    shared_hidden = (jax.nn.silu(shared_gates) * shared_ups).astype(jnp.bfloat16)
    shared = gate_value[:, None] * jnp.dot(shared_hidden, shared_down, preferred_element_type=jnp.float32)
    layer_out = (resid + routed + shared).astype(jnp.bfloat16)
    return (layer_out, new_kv)
```

```python
import functools
import math

import jax
import jax.numpy as jnp
from jax import lax
from jax.experimental import pallas as pl
from jax.experimental.pallas import tpu as pltpu
from jax.sharding import PartitionSpec as P

HD = 128
EXPERTS = 32
FE = 1408
SINKS = 4
CAP = 2
ROWS = 8

EPSILON = 1e-06
ROPE_BASE = 1000000.0
MB = 1 << 20
BF = jnp.bfloat16
F32 = jnp.float32

NT = (((1,), (1,)), ((), ()))


def iota(shape, dim):
    return lax.broadcasted_iota(jnp.int32, shape, dim)


def one(cond):
    return jnp.where(cond, 1.0, 0.0).astype(F32)


def dot(a, b):
    return jnp.dot(a, b, preferred_element_type=F32)


def split3(x):
    hi = x.astype(BF).astype(F32)
    mid = (x - hi).astype(BF).astype(F32)
    lo = (x - hi - mid).astype(BF).astype(F32)
    return jnp.concatenate([hi, mid, lo], axis=0)


def params(limit, **kw):
    return pltpu.CompilerParams(vmem_limit_bytes=limit, **kw)


VM = pl.BlockSpec(memory_space=pltpu.VMEM)
SM = pl.BlockSpec(memory_space=pltpu.SMEM)
HB = pl.BlockSpec(memory_space=pl.ANY)


def attend_kernel(
    groups,
    heads_axis,
    lens,
    hidden,
    gain,
    bias,
    cos,
    sin,
    sink_k,
    sink_v,
    idx,
    rw,
    w_hbm,
    win_hbm,
    ow_hbm,
    part,
    key_out,
    value_out,
    big_out,
    fin_out,
    w_buf,
    kv,
    ow_buf,
    qbd,
    sc,
    wts,
    acc,
    w_sem,
    kv_sem,
    ow_sem,
):
    rows, width = hidden.shape
    local = bias.shape[1]
    length = kv.shape[2]
    chunks = kv_sem.shape[2]
    ch = length // chunks
    halves = w_sem.shape[1]
    wc = width // halves

    def w_copy(c, i):
        return pltpu.make_async_copy(
            w_hbm.at[c, pl.ds(i * wc, wc)], w_buf.at[c, pl.ds(i * wc, wc)], w_sem.at[c, i]
        )

    def kv_copy(r, t, c):
        return pltpu.make_async_copy(
            win_hbm.at[r, t, pl.ds(c * ch, ch)], kv.at[r, t, pl.ds(c * ch, ch)], kv_sem.at[r, t, c]
        )

    def live_of(r):
        return jnp.minimum(lens[r] - SINKS + 1, length)

    def fetch(t):
        def step(r, carry):
            live = live_of(r)
            for c in range(chunks):

                @pl.when(c * ch < live)
                def _():
                    kv_copy(r, t, c).start()

            return carry

        lax.fori_loop(0, rows, step, 0)

    for c in range(3):
        for i in range(halves):
            w_copy(c, i).start()
    fetch(0)
    fetch(1)
    ow_copy = pltpu.make_async_copy(ow_hbm, ow_buf, ow_sem)
    ow_copy.start()

    my_head = lax.axis_index("head")
    local_experts = EXPERTS // groups
    hit = jnp.zeros((rows, EXPERTS), F32)
    comb = jnp.zeros((rows, EXPERTS), F32)
    lane_e = iota((rows, EXPERTS), 1)
    for k in range(idx.shape[1]):
        eq = one(idx[:, k : k + 1] == lane_e)
        hit = hit + eq
        comb = comb + eq * rw[:, k : k + 1]
    below = one(iota((rows, rows), 1) < iota((rows, rows), 0))
    rank = dot(below.astype(BF), hit.astype(BF))
    sel = [hit * one(rank == c) for c in range(CAP)]
    pick = my_head // (heads_axis // local_experts)
    blocks = groups
    span = rows + CAP * blocks
    total = groups * span
    row_g = iota((total, EXPERTS), 0) // span
    row_t = iota((total, EXPERTS), 0) % span
    mine = iota((total, EXPERTS), 1) == row_g * local_experts + pick
    z = jnp.zeros((total, rows), F32)
    for c in range(CAP):
        pickc = mine & (row_t >= rows) & ((row_t - rows) % CAP == c)
        z = z + lax.dot_general(
            one(pickc).astype(BF), sel[c].astype(BF), NT, preferred_element_type=F32
        )
    nb = blocks * rows
    rep = one(iota((rows, nb), 0) == iota((rows, nb), 1) % rows)
    zz = dot(z.astype(BF), rep.astype(BF))
    g2 = iota((total, nb), 0) // span
    t2 = iota((total, nb), 0) % span
    j2 = iota((total, nb), 1) // rows
    r2 = iota((total, nb), 1) % rows
    direct = one((j2 == g2) & (r2 == t2))
    placed = zz * one(j2 == (t2 - rows) // CAP)
    big_out[...] = jnp.where(t2 < rows, direct, placed).astype(BF)

    fin = fin_out.shape[1]
    fspan = fin // (groups * heads_axis)
    ratio = width // heads_axis // (width // groups)
    lane = iota((EXPERTS, fin), 1)
    dev, u = lane // fspan, lane % fspan - rows
    owner = (dev // heads_axis) * local_experts + (dev % heads_axis) // (heads_axis // local_experts)
    spread = jnp.zeros((3 * rows, fin), F32)
    for c in range(CAP):
        hot = (owner == iota((EXPERTS, fin), 0)) & (u >= c * ratio) & (u < (c + 1) * ratio)
        spread = spread + dot(split3(comb * sel[c]).astype(BF), one(hot).astype(BF))
    fin_out[...] = spread.astype(BF)

    x = hidden[...].astype(F32)
    ms = jnp.mean(x * x, axis=-1, keepdims=True)
    normed = (x * lax.rsqrt(ms + EPSILON) * gain[...]).astype(BF)
    proj = []
    for c in range(3):
        total_c = bias[c : c + 1, :]
        for i in range(halves):
            w_copy(c, i).wait()
            total_c = total_c + dot(
                normed[:, i * wc : (i + 1) * wc], w_buf[c, i * wc : (i + 1) * wc, :]
            )
        proj.append(total_c)

    def rotate(v):
        outs = []
        for h in range(local // HD):
            part_h = v[:, h * HD : (h + 1) * HD]
            outs.append(part_h * cos[...] + pltpu.roll(part_h, HD // 2, 1) * sin[...])
        return jnp.concatenate(outs, axis=1)

    q = rotate(proj[0]).astype(BF).astype(F32)
    kf = rotate(proj[1]).astype(BF)
    vf = proj[2].astype(BF)
    key_out[...] = kf
    value_out[...] = vf
    head_mask = iota((ROWS, local), 1) // HD == iota((ROWS, local), 0)
    q3 = jnp.where(head_mask[None], q[:, None, :], 0.0)
    qbd[...] = q3.astype(BF)
    fresh_scores = jnp.sum(q3 * kf.astype(F32)[:, None, :], axis=-1, keepdims=True)

    q_all = q3.reshape(rows * ROWS, local).astype(BF)
    sink_s = lax.dot_general(q_all, sink_k[...], NT, preferred_element_type=F32) / math.sqrt(HD)
    own = iota(sink_s.shape, 1) // SINKS == iota(sink_s.shape, 0) // ROWS
    sink_s = jnp.where(own, sink_s, -jnp.inf)

    def score_step(r, carry):
        used = (live_of(r) + ch - 1) // ch
        for n in range(1, chunks + 1):

            @pl.when(used == n)
            def _():
                for c in range(n):
                    kv_copy(r, 0, c).wait()
                sc[r, :, : n * ch] = lax.dot_general(
                    qbd[r], kv[r, 0, : n * ch, :], NT, preferred_element_type=F32
                )

        return carry

    lax.fori_loop(0, rows, score_step, 0)

    pos = iota((ROWS, length), 1)
    fresh_w, sink_w = [], []
    for r in range(rows):
        slot = lax.rem(lens[r] - SINKS, length)
        is_fresh = pos == slot
        s = jnp.where(is_fresh, fresh_scores[r], sc[r]) / math.sqrt(HD)
        s = jnp.where(pos < live_of(r), s, -jnp.inf)
        ss = sink_s[r * ROWS : (r + 1) * ROWS, :]
        top = jnp.maximum(
            jnp.max(s, axis=-1, keepdims=True), jnp.max(ss, axis=-1, keepdims=True)
        )
        e = jnp.exp(s - top)
        es = jnp.exp(ss - top)
        tot = jnp.sum(e, axis=-1, keepdims=True) + jnp.sum(es, axis=-1, keepdims=True)
        w = (e / tot).astype(BF).astype(F32)
        fresh_w.append(jnp.sum(jnp.where(is_fresh, w, 0.0), axis=-1, keepdims=True))
        sink_w.append(es / tot)
        wts[r] = jnp.where(is_fresh, 0.0, w).astype(BF)

    def value_step(r, carry):
        used = (live_of(r) + ch - 1) // ch
        for n in range(1, chunks + 1):

            @pl.when(used == n)
            def _():
                for c in range(n):
                    kv_copy(r, 1, c).wait()
                acc[r] = dot(wts[r, :, : n * ch], kv[r, 1, : n * ch, :])

        return carry

    lax.fori_loop(0, rows, value_step, 0)

    sink_part = dot(jnp.concatenate(sink_w, axis=0).astype(BF), sink_v[...])
    vf32 = vf.astype(F32)
    attended = []
    for r in range(rows):
        t = acc[r] + sink_part[r * ROWS : (r + 1) * ROWS, :] + fresh_w[r] * vf32[r : r + 1, :]
        attended.append(jnp.sum(jnp.where(head_mask, t, 0.0), axis=0, keepdims=True))
    attended = jnp.concatenate(attended, axis=0).astype(BF)
    ow_copy.wait()
    part[...] = dot(attended, ow_buf[...])


def attend(groups, heads_axis, fspan, lens, hidden, gain, bias, cos, sin, sk, sv, idx, rw, w, win, ow):
    rows, width = hidden.shape
    local = bias.shape[1]
    length = win.shape[2]
    chunks = 4 if length % 4 == 0 else 1
    span = rows + CAP * groups
    return pl.pallas_call(
        functools.partial(attend_kernel, groups, heads_axis),
        out_shape=(
            jax.ShapeDtypeStruct((rows, width), F32),
            jax.ShapeDtypeStruct((rows, local), BF),
            jax.ShapeDtypeStruct((rows, local), BF),
            jax.ShapeDtypeStruct((groups * span, groups * rows), BF),
            jax.ShapeDtypeStruct((3 * rows, groups * heads_axis * fspan), BF),
        ),
        in_specs=[SM] + [VM] * 9 + [HB] * 3,
        out_specs=(VM,) * 5,
        scratch_shapes=[
            pltpu.VMEM((3, width, local), BF),
            pltpu.VMEM((rows, 2, length, local), BF),
            pltpu.VMEM((local, width), BF),
            pltpu.VMEM((rows, ROWS, local), BF),
            pltpu.VMEM((rows, ROWS, length), F32),
            pltpu.VMEM((rows, ROWS, length), BF),
            pltpu.VMEM((rows, ROWS, local), F32),
            pltpu.SemaphoreType.DMA((3, 2)),
            pltpu.SemaphoreType.DMA((rows, 2, chunks)),
            pltpu.SemaphoreType.DMA(()),
        ],
        compiler_params=params(52 * MB),
        name="attend",
    )(lens, hidden, gain, bias, cos, sin, sk, sv, idx, rw, w, win, ow)


def dispatch_kernel(groups, summed, hidden, gain, gate_vec, big, send, gate_out, own_out, keep):
    rows, width = hidden.shape
    resid = hidden[...].astype(F32) + summed[...]
    keep[...] = resid
    ms = jnp.mean(resid * resid, axis=-1, keepdims=True)
    tokens = (resid * lax.rsqrt(ms + EPSILON) * gain[...]).astype(BF).astype(F32)
    gate = jax.nn.sigmoid(jnp.sum(tokens * gate_vec[...], axis=-1, keepdims=True))
    gate_out[...] = jnp.broadcast_to(gate, gate_out.shape)
    w = width // groups
    stacked = jnp.concatenate([tokens[:, j * w : (j + 1) * w] for j in range(groups)], axis=0)
    send[...] = dot(big[...], stacked.astype(BF)).astype(BF)
    slot = own_out.shape[1]
    start = pl.multiple_of(lax.axis_index("head") * slot, HD)
    own_out[...] = keep[:, pl.ds(start, slot)]


def dispatch(groups, slot, summed, hidden, gain, gate_vec, big):
    rows, width = hidden.shape
    return pl.pallas_call(
        functools.partial(dispatch_kernel, groups),
        out_shape=(
            jax.ShapeDtypeStruct((big.shape[0], width // groups), BF),
            jax.ShapeDtypeStruct((rows, HD), F32),
            jax.ShapeDtypeStruct((rows, slot), F32),
        ),
        in_specs=[VM] * 5,
        out_specs=(VM,) * 3,
        scratch_shapes=[pltpu.VMEM((rows, width), F32)],
        compiler_params=params(16 * MB),
        name="dispatch",
    )(summed, hidden, gain, gate_vec, big)


def shared_in_kernel(groups, rows, arrived, weights, out):
    span = arrived.shape[0] // groups
    x = jnp.concatenate(
        [arrived[g * span : g * span + rows, :] for g in range(groups)], axis=0
    )
    f = weights.shape[2]
    out[:, :f] = dot(x, weights[0]).astype(BF)
    out[:, f:] = dot(x, weights[1]).astype(BF)


def shared_in(groups, rows, arrived, weights):
    f = weights.shape[2]
    return pl.pallas_call(
        functools.partial(shared_in_kernel, groups, rows),
        out_shape=jax.ShapeDtypeStruct((groups * rows, 2 * f), BF),
        in_specs=[VM] * 2,
        out_specs=VM,
        compiler_params=params(16 * MB),
        name="shared_in",
    )(arrived, weights)


def shared_act_kernel(groups, sums, out):
    rows = sums.shape[0] // groups
    f = out.shape[1]
    total = sums[0:rows, :].astype(F32)
    for g in range(1, groups):
        total = total + sums[g * rows : (g + 1) * rows, :].astype(F32)
    gate, up = total[:, :f], total[:, f:]
    hidden = (jax.nn.silu(gate) * up).astype(BF)
    for g in range(groups):
        out[g * rows : (g + 1) * rows, :] = hidden


def shared_act(groups, sums):
    f = sums.shape[1] // 2
    return pl.pallas_call(
        functools.partial(shared_act_kernel, groups),
        out_shape=jax.ShapeDtypeStruct((sums.shape[0], f), BF),
        in_specs=[VM],
        out_specs=VM,
        compiler_params=params(16 * MB),
        name="shared_act",
    )(sums)


def expert_kernel(groups, rows, arrived, gu, down, out, xbuf, acc):
    step = pl.program_id(0)
    w = arrived.shape[1]
    slots = groups * CAP

    @pl.when(step == 0)
    def _():
        total = arrived.shape[0]
        span = total // groups
        line, lane = iota((groups * slots, total), 0), iota((groups * slots, total), 1)
        j, g, c = line // slots, line % slots // CAP, line % CAP
        pickm = one(lane == g * span + rows + j * CAP + c).astype(BF)
        x = dot(pickm, arrived[...])
        for jj in range(groups):
            xbuf[:, jj * w : (jj + 1) * w] = x[jj * slots : (jj + 1) * slots, :].astype(BF)
        acc[...] = jnp.zeros_like(acc)

    gate = lax.dot_general(xbuf[...], gu[0], NT, preferred_element_type=F32)
    up = lax.dot_general(xbuf[...], gu[1], NT, preferred_element_type=F32)
    hidden = (jax.nn.silu(gate) * up).astype(BF)
    acc[...] += dot(hidden, down[...])

    @pl.when(step == pl.num_programs(0) - 1)
    def _():
        for jj in range(groups):
            out[jj * slots : (jj + 1) * slots, :] = acc[:, jj * w : (jj + 1) * w].astype(BF)


def experts(groups, rows, arrived, gate_up, down):
    fe, width = down.shape
    piece = 352 if fe % 352 == 0 else fe
    slots = groups * CAP
    total, w = arrived.shape
    return pl.pallas_call(
        functools.partial(expert_kernel, groups, rows),
        out_shape=jax.ShapeDtypeStruct((groups * slots, w), BF),
        grid=(fe // piece,),
        in_specs=[
            pl.BlockSpec((total, w), lambda i: (0, 0)),
            pl.BlockSpec((2, piece, width), lambda i: (0, i, 0)),
            pl.BlockSpec((piece, width), lambda i: (i, 0)),
        ],
        out_specs=pl.BlockSpec((groups * slots, w), lambda i: (0, 0)),
        scratch_shapes=[pltpu.VMEM((slots, width), BF), pltpu.VMEM((slots, width), F32)],
        compiler_params=params(24 * MB, dimension_semantics=("arbitrary",)),
        cost_estimate=pl.CostEstimate(
            flops=6 * slots * fe * width, transcendentals=slots * fe, bytes_accessed=6 * fe * width
        ),
        name="experts",
    )(arrived, gate_up, down)


def give_back_kernel(groups, heads_axis, rows, shared_hidden, down, routed, out):
    shared = dot(shared_hidden[...], down[...]).astype(BF)
    both = jnp.concatenate([shared, routed[...]], axis=0)
    n_shared, n_all = shared.shape[0], both.shape[0]
    total = out.shape[0]
    fspan = total // (groups * heads_axis)
    ratio = groups // heads_axis
    line, lane = iota((total, n_all), 0), iota((total, n_all), 1)
    dev, t = line // fspan, line % fspan
    q, h = dev // heads_axis, dev % heads_axis
    mine = h == lax.axis_index("req") // ratio
    u = t - rows
    j = h * ratio + u % ratio
    target = jnp.where(
        t < rows,
        jnp.where(mine, q * rows + t, -1),
        jnp.where(u < CAP * ratio, n_shared + j * (groups * CAP) + q * CAP + u // ratio, -1),
    )
    out[...] = dot(one(target == lane).astype(BF), both).astype(BF)


def give_back(groups, heads_axis, rows, fspan, shared_hidden, down, routed):
    return pl.pallas_call(
        functools.partial(give_back_kernel, groups, heads_axis, rows),
        out_shape=jax.ShapeDtypeStruct((groups * heads_axis * fspan, down.shape[1]), BF),
        in_specs=[VM] * 3,
        out_specs=VM,
        compiler_params=params(16 * MB),
        name="give_back",
    )(shared_hidden, down, routed)


def finish_kernel(groups, heads_axis, returned, fin, gate, own, out):
    rows = own.shape[0]
    w = returned.shape[1]
    ratio = groups // heads_axis
    total = returned.shape[0]
    fspan = total // (groups * heads_axis)
    my_head = lax.axis_index("head")
    line, lane = iota((3 * rows, total), 0) % rows, iota((3 * rows, total), 1)
    q, t = lane // (fspan * heads_axis), lane % fspan
    gate3 = split3(gate[:, 0:1])
    base = fin[...].astype(F32)
    for p in range(ratio):
        routed_w = jnp.where((t - rows) % ratio == p, base, 0.0)
        shared_w = jnp.where((t == line) & (q == my_head * ratio + p), gate3, 0.0)
        weight = jnp.where(t < rows, shared_w, routed_w)
        terms = dot(weight.astype(BF), returned[...])
        value = terms[:rows] + terms[rows : 2 * rows] + terms[2 * rows :]
        out[:, p * w : (p + 1) * w] = (own[:, p * w : (p + 1) * w] + value).astype(BF)


def finish(groups, heads_axis, returned, fin, gate, own):
    return pl.pallas_call(
        functools.partial(finish_kernel, groups, heads_axis),
        out_shape=jax.ShapeDtypeStruct(own.shape, BF),
        in_specs=[VM] * 4,
        out_specs=VM,
        compiler_params=params(16 * MB),
        name="finish",
    )(returned, fin, gate, own)


def local(
    hidden_state,
    attend_gain,
    input_weight,
    input_bias,
    output_weight,
    window_cache,
    sink_cache,
    lengths,
    expert_index,
    router_weight,
    mixture_gain,
    expert_gate_up,
    expert_down,
    shared_gate_up,
    shared_down,
    shared_gate,
):
    rows, width = hidden_state.shape
    local_width = input_weight.shape[2]
    groups = lax.axis_size("req")
    heads_axis = lax.axis_size("head")
    slot = width // heads_axis
    fspan = 16

    half = HD // 2
    frequencies = F32(ROPE_BASE) ** (-(2.0 / HD) * jnp.arange(half).astype(F32))
    angles = lengths.astype(F32)[:, None] * frequencies[None, :]
    cosine, sine = jnp.cos(angles), jnp.sin(angles)
    cos = jnp.concatenate([cosine, cosine], axis=1)
    sin = jnp.concatenate([-sine, sine], axis=1)
    sink_k = sink_cache[:, 0].reshape(rows * SINKS, local_width)
    sink_v = sink_cache[:, 1].reshape(rows * SINKS, local_width)

    part, key, value, big, fin = attend(
        groups,
        heads_axis,
        fspan,
        lengths,
        hidden_state,
        attend_gain[None],
        input_bias,
        cos,
        sin,
        sink_k,
        sink_v,
        expert_index,
        router_weight,
        jnp.transpose(input_weight, (1, 0, 2)),
        window_cache,
        output_weight,
    )
    new_kv = jnp.stack([key, value], axis=1)
    summed = part
    bit = 1
    while bit < heads_axis:
        summed = summed + lax.ppermute(
            summed, "head", [(j, j ^ bit) for j in range(heads_axis)]
        )
        bit *= 2

    send, gate, own = dispatch(
        groups, slot, summed, hidden_state, mixture_gain[None], shared_gate[None], big
    )
    arrived = lax.all_to_all(send, "req", split_axis=0, concat_axis=0, tiled=True)
    sums = shared_in(groups, rows, arrived, shared_gate_up)
    sums = lax.all_to_all(sums, "req", split_axis=0, concat_axis=0, tiled=True)
    routed = experts(groups, rows, arrived, expert_gate_up, expert_down)
    shared_hidden = shared_act(groups, sums)
    shared_hidden = lax.all_to_all(shared_hidden, "req", split_axis=0, concat_axis=0, tiled=True)
    back = give_back(groups, heads_axis, rows, fspan, shared_hidden, shared_down, routed)
    returned = lax.all_to_all(back, ("req", "head"), split_axis=0, concat_axis=0, tiled=True)
    return finish(groups, heads_axis, returned, fin, gate, own), new_kv


def solution(mesh):
    return jax.shard_map(
        local,
        mesh=mesh,
        in_specs=(
            P("req", None),
            P(),
            P(None, None, "head"),
            P(None, "head"),
            P("head", None),
            P("req", None, None, "head"),
            P("req", None, None, "head"),
            P("req"),
            P("req", None),
            P("req", None),
            P(),
            P(None, ("req", "head"), None),
            P(("req", "head"), None),
            P(None, "req", "head"),
            P("head", "req"),
            P(),
        ),
        out_specs=(P("req", "head"), P("req", None, "head")),
        check_vma=False,
    )
```

```python
import functools
import math

import jax
import jax.numpy as jnp
from jax import lax
from jax.experimental import pallas as pl
from jax.experimental.pallas import tpu as pltpu
from jax.sharding import PartitionSpec as P

HD = 128
EXPERTS = 32
FE = 1408
SINKS = 4
CAP = 2
ROWS = 8

EPSILON = 1e-06
ROPE_BASE = 1000000.0
MB = 1 << 20
BF = jnp.bfloat16
F32 = jnp.float32


def stay(x):
    return pltpu.with_memory_space_constraint(x, pltpu.HBM)


NT = (((1,), (1,)), ((), ()))


def iota(shape, dim):
    return lax.broadcasted_iota(jnp.int32, shape, dim)


def one(cond):
    return jnp.where(cond, 1.0, 0.0).astype(F32)


def dot(a, b):
    return jnp.dot(a, b, preferred_element_type=F32)


def split3(x):
    hi = x.astype(BF).astype(F32)
    mid = (x - hi).astype(BF).astype(F32)
    lo = (x - hi - mid).astype(BF).astype(F32)
    return hi, mid, lo


def params(limit, **kw):
    return pltpu.CompilerParams(vmem_limit_bytes=limit, **kw)


VM = pl.BlockSpec(memory_space=pltpu.VMEM)
SM = pl.BlockSpec(memory_space=pltpu.SMEM)
HB = pl.BlockSpec(memory_space=pltpu.HBM)


def routing_tables(groups, heads_axis, idx, rw, big_out, meta_out):
    rows = idx.shape[1]
    local_experts = EXPERTS // groups
    pick = lax.axis_index("head") // (heads_axis // local_experts)
    hit = jnp.zeros((EXPERTS, rows), F32)
    comb = jnp.zeros((EXPERTS, rows), F32)
    line_e = iota((EXPERTS, rows), 0)
    for k in range(idx.shape[0]):
        eq = one(idx[k : k + 1, :] == line_e)
        hit = hit + eq
        comb = comb + eq * rw[k : k + 1, :]
    above = one(iota((rows, rows), 0) < iota((rows, rows), 1))
    rank = dot(hit.astype(BF), above.astype(BF))
    sel = [hit * one(rank == c) for c in range(CAP)]
    span = rows + CAP * groups
    total = groups * span
    row_g = iota((total, EXPERTS), 0) // span
    row_t = iota((total, EXPERTS), 0) % span
    mine = iota((total, EXPERTS), 1) == row_g * local_experts + pick
    z = jnp.zeros((total, rows), F32)
    for c in range(CAP):
        pickc = mine & (row_t >= rows) & ((row_t - rows) % CAP == c)
        z = z + dot(one(pickc).astype(BF), sel[c].astype(BF))
    nb = groups * rows
    rep = one(iota((rows, nb), 0) == iota((rows, nb), 1) % rows)
    zz = dot(z.astype(BF), rep.astype(BF))
    g2 = iota((total, nb), 0) // span
    t2 = iota((total, nb), 0) % span
    j2 = iota((total, nb), 1) // rows
    r2 = iota((total, nb), 1) % rows
    direct = one((j2 == g2) & (r2 == t2))
    placed = zz * one(j2 == (t2 - rows) // CAP)
    big_out[...] = jnp.where(t2 < rows, direct, placed).astype(BF)

    w = meta_out.shape[1]
    again = one(iota((nb, rows), 0) % rows == iota((nb, rows), 1)).astype(BF)
    keep = iota((nb, EXPERTS), 1) == (iota((nb, EXPERTS), 0) // rows) * local_experts + pick
    meta = jnp.zeros((nb, w), F32)
    for c in range(CAP):
        for p, term in enumerate(split3(comb * sel[c])):
            wide = lax.dot_general(again, term.astype(BF), NT, preferred_element_type=F32)
            wide = jnp.where(keep, wide, 0.0).astype(BF)
            column = one(iota((EXPERTS, w), 1) == 3 * c + p).astype(BF)
            meta = meta + dot(wide, column)
    meta_out[...] = meta.astype(BF)


def attend_kernel(
    groups,
    heads_axis,
    freq,
    lens_hbm,
    hidden_hbm,
    gain_hbm,
    bias_hbm,
    sink_hbm,
    idx_hbm,
    rw_hbm,
    w_hbm,
    win_hbm,
    ow_hbm,
    part,
    key_out,
    value_out,
    big_out,
    meta_out,
    lens,
    hidden,
    gain,
    bias,
    sink,
    idx,
    rw,
    w_buf,
    kv,
    ow_buf,
    qbd,
    sc,
    wts,
    acc,
    small_sem,
    w_sem,
    kv_sem,
    ow_sem,
):
    rows, width = hidden.shape
    local = bias.shape[1]
    length = kv.shape[2]
    chunks = kv_sem.shape[2]
    ch = length // chunks
    halves = w_sem.shape[1]
    wc = width // halves

    small = [
        pltpu.make_async_copy(src, dst, small_sem.at[i])
        for i, (src, dst) in enumerate(
            (
                (lens_hbm, lens),
                (hidden_hbm, hidden),
                (gain_hbm, gain),
                (bias_hbm, bias),
                (idx_hbm, idx),
                (rw_hbm, rw),
                (sink_hbm, sink),
            )
        )
    ]

    def w_copy(c, i):
        return pltpu.make_async_copy(
            w_hbm.at[c, pl.ds(i * wc, wc)], w_buf.at[c, pl.ds(i * wc, wc)], w_sem.at[c, i]
        )

    def kv_copy(r, t, c):
        return pltpu.make_async_copy(
            win_hbm.at[r, t, pl.ds(c * ch, ch)], kv.at[r, t, pl.ds(c * ch, ch)], kv_sem.at[r, t, c]
        )

    def live_of(r):
        return jnp.minimum(lens[r] - SINKS + 1, length)

    def fetch(t):
        def step(r, carry):
            live = live_of(r)
            for c in range(chunks):

                @pl.when(c * ch < live)
                def _():
                    kv_copy(r, t, c).start()

            return carry

        lax.fori_loop(0, rows, step, 0)

    for copy in small:
        copy.start()
    for c in range(3):
        for i in range(halves):
            w_copy(c, i).start()
    small[0].wait()
    fetch(0)
    fetch(1)
    ow_copy = pltpu.make_async_copy(ow_hbm, ow_buf, ow_sem)
    ow_copy.start()
    for copy in small[1:]:
        copy.wait()

    routing_tables(groups, heads_axis, idx, rw, big_out, meta_out)

    place = jnp.concatenate([jnp.full((1, HD // 2), lens[r], jnp.int32) for r in range(rows)], axis=0)
    angles = place.astype(F32) * freq[...]
    cosine, sine = jnp.cos(angles), jnp.sin(angles)
    cos = jnp.concatenate([cosine, cosine], axis=1)
    sin = jnp.concatenate([-sine, sine], axis=1)

    x = hidden[...].astype(F32)
    ms = jnp.mean(x * x, axis=-1, keepdims=True)
    normed = (x * lax.rsqrt(ms + EPSILON) * gain[...]).astype(BF)
    proj = []
    for c in range(3):
        total_c = bias[c : c + 1, :]
        for i in range(halves):
            w_copy(c, i).wait()
            total_c = total_c + dot(
                normed[:, i * wc : (i + 1) * wc], w_buf[c, i * wc : (i + 1) * wc, :]
            )
        proj.append(total_c)

    def rotate(v):
        outs = []
        for h in range(local // HD):
            part_h = v[:, h * HD : (h + 1) * HD]
            outs.append(part_h * cos + pltpu.roll(part_h, HD // 2, 1) * sin)
        return jnp.concatenate(outs, axis=1)

    q = rotate(proj[0]).astype(BF).astype(F32)
    kf = rotate(proj[1]).astype(BF)
    vf = proj[2].astype(BF)
    key_out[...] = kf
    value_out[...] = vf
    head_mask = iota((ROWS, local), 1) // HD == iota((ROWS, local), 0)
    q3 = jnp.where(head_mask[None], q[:, None, :], 0.0)
    qbd[...] = q3.astype(BF)
    fresh_scores = jnp.sum(q3 * kf.astype(F32)[:, None, :], axis=-1, keepdims=True)

    sink_s = [
        lax.dot_general(qbd[r], sink[r, 0], NT, preferred_element_type=F32) / math.sqrt(HD)
        for r in range(rows)
    ]

    def score_step(r, carry):
        used = (live_of(r) + ch - 1) // ch
        for n in range(1, chunks + 1):

            @pl.when(used == n)
            def _():
                for c in range(n):
                    kv_copy(r, 0, c).wait()
                sc[r, :, : n * ch] = lax.dot_general(
                    qbd[r], kv[r, 0, : n * ch, :], NT, preferred_element_type=F32
                )

        return carry

    lax.fori_loop(0, rows, score_step, 0)

    pos = iota((ROWS, length), 1)
    rest = []
    vf32 = vf.astype(F32)
    for r in range(rows):
        slot = lax.rem(lens[r] - SINKS, length)
        is_fresh = pos == slot
        s = jnp.where(is_fresh, fresh_scores[r], sc[r]) / math.sqrt(HD)
        s = jnp.where(pos < live_of(r), s, -jnp.inf)
        ss = sink_s[r]
        top = jnp.maximum(
            jnp.max(s, axis=-1, keepdims=True), jnp.max(ss, axis=-1, keepdims=True)
        )
        e = jnp.exp(s - top)
        es = jnp.exp(ss - top)
        tot = jnp.sum(e, axis=-1, keepdims=True) + jnp.sum(es, axis=-1, keepdims=True)
        w = (e / tot).astype(BF).astype(F32)
        fresh_w = jnp.sum(jnp.where(is_fresh, w, 0.0), axis=-1, keepdims=True)
        rest.append(fresh_w * vf32[r : r + 1, :] + dot((es / tot).astype(BF), sink[r, 1]))
        wts[r] = jnp.where(is_fresh, 0.0, w).astype(BF)

    def value_step(r, carry):
        used = (live_of(r) + ch - 1) // ch
        for n in range(1, chunks + 1):

            @pl.when(used == n)
            def _():
                for c in range(n):
                    kv_copy(r, 1, c).wait()
                acc[r] = dot(wts[r, :, : n * ch], kv[r, 1, : n * ch, :])

        return carry

    lax.fori_loop(0, rows, value_step, 0)

    attended = [
        jnp.sum(jnp.where(head_mask, acc[r] + rest[r], 0.0), axis=0, keepdims=True)
        for r in range(rows)
    ]
    attended = jnp.concatenate(attended, axis=0).astype(BF)
    ow_copy.wait()
    part[...] = dot(attended, ow_buf[...])


def attend(groups, heads_axis, freq, lens, hidden, gain, bias, sink, idx, rw, w, win, ow):
    rows, width = hidden.shape
    local = bias.shape[1]
    length = win.shape[2]
    chunks = 4 if length % 4 == 0 else 1
    span = rows + CAP * groups
    return pl.pallas_call(
        functools.partial(attend_kernel, groups, heads_axis),
        out_shape=(
            jax.ShapeDtypeStruct((rows, width), F32),
            jax.ShapeDtypeStruct((rows, local), BF),
            jax.ShapeDtypeStruct((rows, local), BF),
            jax.ShapeDtypeStruct((groups * span, groups * rows), BF),
            jax.ShapeDtypeStruct((groups * rows, width // groups), BF),
        ),
        in_specs=[VM] + [HB] * 10,
        out_specs=(VM,) * 5,
        scratch_shapes=[
            pltpu.SMEM(lens.shape, lens.dtype),
            pltpu.VMEM(hidden.shape, hidden.dtype),
            pltpu.VMEM(gain.shape, gain.dtype),
            pltpu.VMEM(bias.shape, bias.dtype),
            pltpu.VMEM(sink.shape, sink.dtype),
            pltpu.VMEM(idx.shape, idx.dtype),
            pltpu.VMEM(rw.shape, rw.dtype),
            pltpu.VMEM((3, width, local), BF),
            pltpu.VMEM((rows, 2, length, local), BF),
            pltpu.VMEM((local, width), BF),
            pltpu.VMEM((rows, ROWS, local), BF),
            pltpu.VMEM((rows, ROWS, length), F32),
            pltpu.VMEM((rows, ROWS, length), BF),
            pltpu.VMEM((rows, ROWS, local), F32),
            pltpu.SemaphoreType.DMA((7,)),
            pltpu.SemaphoreType.DMA((3, 2)),
            pltpu.SemaphoreType.DMA((rows, 2, chunks)),
            pltpu.SemaphoreType.DMA(()),
        ],
        compiler_params=params(52 * MB),
        name="attend",
    )(freq, *map(stay, (lens, hidden, gain, bias, sink, idx, rw, w, win, ow)))


def dispatch_kernel(groups, summed, hidden, gain, gate_vec, big, meta, send, own_out, keep):
    rows, width = hidden.shape
    resid = hidden[...].astype(F32) + summed[...]
    keep[...] = resid
    ms = jnp.mean(resid * resid, axis=-1, keepdims=True)
    tokens = (resid * lax.rsqrt(ms + EPSILON) * gain[...]).astype(BF).astype(F32)
    gate = jax.nn.sigmoid(jnp.sum(tokens * gate_vec[...], axis=-1, keepdims=True))
    w = width // groups
    stacked = jnp.concatenate([tokens[:, j * w : (j + 1) * w] for j in range(groups)], axis=0)
    placed = dot(big[...], stacked.astype(BF)).astype(BF)
    lane = iota((rows, w), 1)
    extra = jnp.zeros((rows, w), F32)
    for p, term in enumerate(split3(gate)):
        extra = extra + jnp.where(lane == 3 * CAP + p, term, 0.0)
    span = placed.shape[0] // groups
    full = send.shape[0] // groups
    for g in range(groups):
        send[g * full : g * full + span, :] = placed[g * span : (g + 1) * span, :]
        told = meta[g * rows : (g + 1) * rows, :].astype(F32) + extra
        send[g * full + span : (g + 1) * full, :] = told.astype(BF)
    slot = own_out.shape[1]
    start = pl.multiple_of(lax.axis_index("head") * slot, HD)
    own_out[...] = keep[:, pl.ds(start, slot)]


def dispatch(groups, slot, summed, hidden, gain, gate_vec, big, meta):
    rows, width = hidden.shape
    return pl.pallas_call(
        functools.partial(dispatch_kernel, groups),
        out_shape=(
            jax.ShapeDtypeStruct((big.shape[0] + groups * rows, width // groups), BF),
            jax.ShapeDtypeStruct((rows, slot), F32),
        ),
        in_specs=[VM] * 6,
        out_specs=(VM,) * 2,
        scratch_shapes=[pltpu.VMEM((rows, width), F32)],
        compiler_params=params(16 * MB),
        name="dispatch",
    )(summed, hidden, gain, gate_vec, big, meta)


def shared_in_kernel(groups, rows, arrived, weights, out):
    span = arrived.shape[0] // groups
    x = jnp.concatenate(
        [arrived[g * span : g * span + rows, :] for g in range(groups)], axis=0
    )
    tokens = x.shape[0]
    both = jnp.concatenate([dot(x, weights[0]), dot(x, weights[1])], axis=0)
    out[...] = both.T.astype(BF)


def shared_in(groups, rows, arrived, weights):
    return pl.pallas_call(
        functools.partial(shared_in_kernel, groups, rows),
        out_shape=jax.ShapeDtypeStruct((weights.shape[2], 2 * groups * rows), BF),
        in_specs=[VM] * 2,
        out_specs=VM,
        compiler_params=params(16 * MB),
        name="shared_in",
    )(arrived, weights)


def expert_kernel(groups, rows, arrived, gu_hbm, down_hbm, out, gu, down, gu_sem, down_sem):
    pieces = down_sem.shape[0]
    piece = down.shape[0] // pieces

    def gu_copy(t, i):
        at = pl.ds(i * piece, piece)
        return pltpu.make_async_copy(gu_hbm.at[t, at], gu.at[t, at], gu_sem.at[t, i])

    def down_copy(i):
        at = pl.ds(i * piece, piece)
        return pltpu.make_async_copy(down_hbm.at[at], down.at[at], down_sem.at[i])

    for i in range(pieces):
        gu_copy(0, i).start()
        gu_copy(1, i).start()
        down_copy(i).start()

    slots = groups * CAP
    total = arrived.shape[0]
    span = total // groups
    line, lane = iota((groups * slots, total), 0), iota((groups * slots, total), 1)
    j, g, c = line // slots, line % slots // CAP, line % CAP
    pickm = one(lane == g * span + rows + j * CAP + c).astype(BF)
    x = dot(pickm, arrived[...])
    x = jnp.concatenate(
        [x[jj * slots : (jj + 1) * slots, :] for jj in range(groups)], axis=1
    ).astype(BF)
    result = jnp.zeros((slots, down.shape[1]), F32)
    for i in range(pieces):
        at = slice(i * piece, (i + 1) * piece)
        gu_copy(0, i).wait()
        gate = lax.dot_general(x, gu[0, at, :], NT, preferred_element_type=F32)
        gu_copy(1, i).wait()
        up = lax.dot_general(x, gu[1, at, :], NT, preferred_element_type=F32)
        hidden = (jax.nn.silu(gate) * up).astype(BF)
        down_copy(i).wait()
        result = result + dot(hidden, down[at, :])
    out[...] = result


def experts(groups, rows, arrived, gate_up, down):
    fe, width = down.shape
    pieces = fe // 352 if fe % 352 == 0 else 1
    slots = groups * CAP
    return pl.pallas_call(
        functools.partial(expert_kernel, groups, rows),
        out_shape=jax.ShapeDtypeStruct((slots, width), F32),
        in_specs=[VM, HB, HB],
        out_specs=VM,
        scratch_shapes=[
            pltpu.VMEM(gate_up.shape, BF),
            pltpu.VMEM(down.shape, BF),
            pltpu.SemaphoreType.DMA((2, pieces)),
            pltpu.SemaphoreType.DMA((pieces,)),
        ],
        compiler_params=params(32 * MB),
        cost_estimate=pl.CostEstimate(
            flops=6 * slots * fe * width, transcendentals=slots * fe, bytes_accessed=6 * fe * width
        ),
        name="experts",
    )(arrived, stay(gate_up), stay(down))


def give_back_kernel(groups, heads_axis, rows, sums, down, routed, arrived, out):
    total = sums[0].astype(F32)
    for g in range(1, groups):
        total = total + sums[g].astype(F32)
    tokens = groups * rows
    hidden = jax.nn.silu(total) * pltpu.roll(total, tokens, 1)
    hidden = hidden[:, :tokens].T.astype(BF)
    span = arrived.shape[0] // groups
    told = jnp.concatenate(
        [arrived[(g + 1) * span - rows : (g + 1) * span, :HD] for g in range(groups)], axis=0
    ).astype(F32)

    def column(k):
        return told[:, 3 * k : 3 * k + 1] + told[:, 3 * k + 1 : 3 * k + 2] + told[:, 3 * k + 2 : 3 * k + 3]

    gate = column(CAP)
    weight = [column(c) for c in range(CAP)]
    w = down.shape[2]
    ratio = groups // heads_axis
    for j in range(groups):
        shared = gate * dot(hidden, down[j])
        h, half = j // ratio, j % ratio
        for g in range(groups):
            at = slice(g * rows, (g + 1) * rows)
            value = shared[at]
            for c in range(CAP):
                line = routed[g * CAP + c : g * CAP + c + 1, j * w : (j + 1) * w]
                value = value + weight[c][at] * line
            to = (g * heads_axis + h) * rows
            out[to : to + rows, half * w : (half + 1) * w] = value.astype(BF)


def give_back(groups, heads_axis, rows, sums, down, routed, arrived):
    return pl.pallas_call(
        functools.partial(give_back_kernel, groups, heads_axis, rows),
        out_shape=jax.ShapeDtypeStruct(
            (groups * heads_axis * rows, routed.shape[1] // heads_axis), BF
        ),
        in_specs=[VM] * 4,
        out_specs=VM,
        compiler_params=params(16 * MB),
        name="give_back",
    )(sums, down, routed, arrived)


def finish_kernel(returned, own, out):
    rows = own.shape[0]
    total = own[...]
    for i in range(returned.shape[0] // rows):
        total = total + returned[i * rows : (i + 1) * rows, :].astype(F32)
    out[...] = total.astype(BF)


def finish(returned, own):
    return pl.pallas_call(
        finish_kernel,
        out_shape=jax.ShapeDtypeStruct(own.shape, BF),
        in_specs=[VM] * 2,
        out_specs=VM,
        compiler_params=params(16 * MB),
        name="finish",
    )(returned, own)


def local(
    hidden_state,
    attend_gain,
    input_weight,
    input_bias,
    output_weight,
    window_cache,
    sink_cache,
    lengths,
    expert_index,
    router_weight,
    mixture_gain,
    expert_gate_up,
    expert_down,
    shared_gate_up,
    shared_down,
    shared_gate,
):
    rows, width = hidden_state.shape
    local_width = input_weight.shape[2]
    groups = lax.axis_size("req")
    heads_axis = lax.axis_size("head")
    slot = width // heads_axis
    half = HD // 2
    frequencies = F32(ROPE_BASE) ** (-(2.0 / HD) * jnp.arange(half).astype(F32))
    down = shared_down.reshape(groups, shared_down.shape[0] // groups, shared_down.shape[1])
    down = lax.all_to_all(down, "req", split_axis=0, concat_axis=0, tiled=True)

    part, key, value, big, meta = attend(
        groups,
        heads_axis,
        frequencies[None],
        lengths,
        hidden_state,
        attend_gain[None],
        input_bias,
        sink_cache,
        expert_index.T,
        router_weight.T,
        jnp.transpose(input_weight, (1, 0, 2)),
        window_cache,
        output_weight,
    )
    new_kv = jnp.stack([key, value], axis=1)
    summed = part
    bit = 1
    while bit < heads_axis:
        summed = summed + lax.ppermute(
            summed, "head", [(j, j ^ bit) for j in range(heads_axis)]
        )
        bit *= 2

    summed, down = lax.optimization_barrier((summed, down))
    send, own = dispatch(
        groups, slot, summed, hidden_state, mixture_gain[None], shared_gate[None], big, meta
    )
    arrived = lax.all_to_all(send, "req", split_axis=0, concat_axis=0, tiled=True)
    sums = shared_in(groups, rows, arrived, shared_gate_up)
    sums = sums.reshape(groups, sums.shape[0] // groups, sums.shape[1])
    sums = lax.all_to_all(sums, "req", split_axis=0, concat_axis=0, tiled=True)
    routed = experts(groups, rows, arrived, expert_gate_up, expert_down)
    back = give_back(groups, heads_axis, rows, sums, down, routed, arrived)
    returned = lax.all_to_all(back, ("req", "head"), split_axis=0, concat_axis=0, tiled=True)
    return finish(returned, own), new_kv


def solution(mesh):
    return jax.shard_map(
        local,
        mesh=mesh,
        in_specs=(
            P("req", None),
            P(),
            P(None, None, "head"),
            P(None, "head"),
            P("head", None),
            P("req", None, None, "head"),
            P("req", None, None, "head"),
            P("req"),
            P("req", None),
            P("req", None),
            P(),
            P(None, ("req", "head"), None),
            P(("req", "head"), None),
            P(None, "req", "head"),
            P("head", "req"),
            P(),
        ),
        out_specs=(P("req", "head"), P("req", None, "head")),
        check_vma=False,
    )
```

```python
import functools
import math

import jax
import jax.numpy as jnp
from jax import lax
from jax.experimental import pallas as pl
from jax.experimental.pallas import tpu as pltpu
from jax.sharding import PartitionSpec as P

HD = 128
EXPERTS = 32
FE = 1408
SINKS = 4
CAP = 2
ROWS = 8

EPSILON = 1e-06
ROPE_BASE = 1000000.0
MB = 1 << 20
SPAN = 384
BF = jnp.bfloat16
F32 = jnp.float32


def stay(x):
    return pltpu.with_memory_space_constraint(x, pltpu.HBM)


NT = (((1,), (1,)), ((), ()))


def iota(shape, dim):
    return lax.broadcasted_iota(jnp.int32, shape, dim)


def one(cond):
    return jnp.where(cond, 1.0, 0.0).astype(F32)


def dot(a, b):
    return jnp.dot(a, b, preferred_element_type=F32)


def split3(x):
    hi = x.astype(BF).astype(F32)
    mid = (x - hi).astype(BF).astype(F32)
    lo = (x - hi - mid).astype(BF).astype(F32)
    return hi, mid, lo


def params(limit, **kw):
    return pltpu.CompilerParams(vmem_limit_bytes=limit, **kw)


VM = pl.BlockSpec(memory_space=pltpu.VMEM)
SM = pl.BlockSpec(memory_space=pltpu.SMEM)
HB = pl.BlockSpec(memory_space=pltpu.HBM)


def routing_tables(groups, heads_axis, idx, rw, big_out, meta_out):
    rows = idx.shape[1]
    local_experts = EXPERTS // groups
    pick = lax.axis_index("head") // (heads_axis // local_experts)
    hit = jnp.zeros((EXPERTS, rows), F32)
    comb = jnp.zeros((EXPERTS, rows), F32)
    line_e = iota((EXPERTS, rows), 0)
    for k in range(idx.shape[0]):
        eq = one(idx[k : k + 1, :] == line_e)
        hit = hit + eq
        comb = comb + eq * rw[k : k + 1, :]
    above = one(iota((rows, rows), 0) < iota((rows, rows), 1))
    rank = dot(hit.astype(BF), above.astype(BF))
    sel = [hit * one(rank == c) for c in range(CAP)]
    span = rows + CAP * groups
    total = groups * span
    row_g = iota((total, EXPERTS), 0) // span
    row_t = iota((total, EXPERTS), 0) % span
    mine = iota((total, EXPERTS), 1) == row_g * local_experts + pick
    z = jnp.zeros((total, rows), F32)
    for c in range(CAP):
        pickc = mine & (row_t >= rows) & ((row_t - rows) % CAP == c)
        z = z + dot(one(pickc).astype(BF), sel[c].astype(BF))
    nb = groups * rows
    rep = one(iota((rows, nb), 0) == iota((rows, nb), 1) % rows)
    zz = dot(z.astype(BF), rep.astype(BF))
    g2 = iota((total, nb), 0) // span
    t2 = iota((total, nb), 0) % span
    j2 = iota((total, nb), 1) // rows
    r2 = iota((total, nb), 1) % rows
    direct = one((j2 == g2) & (r2 == t2))
    placed = zz * one(j2 == (t2 - rows) // CAP)
    big_out[...] = jnp.where(t2 < rows, direct, placed).astype(BF)

    w = meta_out.shape[1]
    again = one(iota((nb, rows), 0) % rows == iota((nb, rows), 1)).astype(BF)
    keep = iota((nb, EXPERTS), 1) == (iota((nb, EXPERTS), 0) // rows) * local_experts + pick
    meta = jnp.zeros((nb, w), F32)
    for c in range(CAP):
        for p, term in enumerate(split3(comb * sel[c])):
            wide = lax.dot_general(again, term.astype(BF), NT, preferred_element_type=F32)
            wide = jnp.where(keep, wide, 0.0).astype(BF)
            column = one(iota((EXPERTS, w), 1) == 3 * c + p).astype(BF)
            meta = meta + dot(wide, column)
    meta_out[...] = meta.astype(BF)


def attend_kernel(
    groups,
    heads_axis,
    freq,
    lens_hbm,
    hidden_hbm,
    gain_hbm,
    bias_hbm,
    sink_hbm,
    idx_hbm,
    rw_hbm,
    w_hbm,
    win_hbm,
    ow_hbm,
    part,
    part_low,
    new_kv,
    big_out,
    meta_out,
    lens,
    hidden,
    gain,
    bias,
    sink,
    idx,
    rw,
    w_buf,
    kv,
    ow_buf,
    qbd,
    sc,
    wts,
    acc,
    small_sem,
    w_sem,
    kv_sem,
    ow_sem,
):
    rows, width = hidden.shape
    local = bias.shape[1]
    length = kv.shape[2]
    chunks = kv_sem.shape[2]
    ch = length // chunks
    halves = w_sem.shape[1]
    wc = width // halves

    small = [
        pltpu.make_async_copy(src, dst, small_sem.at[i])
        for i, (src, dst) in enumerate(
            (
                (lens_hbm, lens),
                (hidden_hbm, hidden),
                (gain_hbm, gain),
                (bias_hbm, bias),
                (idx_hbm, idx),
                (rw_hbm, rw),
                (sink_hbm, sink),
            )
        )
    ]

    def w_copy(c, i):
        return pltpu.make_async_copy(
            w_hbm.at[c, pl.ds(i * wc, wc)], w_buf.at[c, pl.ds(i * wc, wc)], w_sem.at[c, i]
        )

    def kv_copy(r, t, c):
        return pltpu.make_async_copy(
            win_hbm.at[r, t, pl.ds(c * ch, ch)], kv.at[r, t, pl.ds(c * ch, ch)], kv_sem.at[r, t, c]
        )

    def live_of(r):
        return jnp.minimum(lens[r] - SINKS + 1, length)

    def fetch(t):
        def step(r, carry):
            live = live_of(r)
            for c in range(chunks):

                @pl.when(c * ch < live)
                def _():
                    kv_copy(r, t, c).start()

            return carry

        lax.fori_loop(0, rows, step, 0)

    for copy in small:
        copy.start()
    for c in range(3):
        for i in range(halves):
            w_copy(c, i).start()
    small[0].wait()
    fetch(0)
    fetch(1)
    ow_copy = pltpu.make_async_copy(ow_hbm, ow_buf, ow_sem)
    ow_copy.start()
    for copy in small[1:]:
        copy.wait()

    routing_tables(groups, heads_axis, idx, rw, big_out, meta_out)

    place = jnp.concatenate([jnp.full((1, HD // 2), lens[r], jnp.int32) for r in range(rows)], axis=0)
    angles = place.astype(F32) * freq[...]
    cosine, sine = jnp.cos(angles), jnp.sin(angles)
    cos = jnp.concatenate([cosine, cosine], axis=1)
    sin = jnp.concatenate([-sine, sine], axis=1)

    x = hidden[...].astype(F32)
    ms = jnp.mean(x * x, axis=-1, keepdims=True)
    normed = (x * lax.rsqrt(ms + EPSILON) * gain[...]).astype(BF)
    proj = []
    for c in range(3):
        total_c = bias[c : c + 1, :]
        for i in range(halves):
            w_copy(c, i).wait()
            total_c = total_c + dot(
                normed[:, i * wc : (i + 1) * wc], w_buf[c, i * wc : (i + 1) * wc, :]
            )
        proj.append(total_c)

    def rotate(v):
        outs = []
        for h in range(local // HD):
            part_h = v[:, h * HD : (h + 1) * HD]
            outs.append(part_h * cos + pltpu.roll(part_h, HD // 2, 1) * sin)
        return jnp.concatenate(outs, axis=1)

    q = rotate(proj[0]).astype(BF).astype(F32)
    kf = rotate(proj[1]).astype(BF)
    vf = proj[2].astype(BF)
    new_kv[...] = jnp.stack([kf.astype(F32), vf.astype(F32)], axis=1).astype(BF)
    head_mask = iota((ROWS, local), 1) // HD == iota((ROWS, local), 0)
    q3 = jnp.where(head_mask[None], q[:, None, :], 0.0)
    qbd[...] = q3.astype(BF)
    fresh_scores = jnp.sum(q3 * kf.astype(F32)[:, None, :], axis=-1, keepdims=True)

    sink_s = [
        lax.dot_general(qbd[r], sink[r, 0], NT, preferred_element_type=F32) / math.sqrt(HD)
        for r in range(rows)
    ]

    def score_step(r, carry):
        used = (live_of(r) + ch - 1) // ch
        for n in range(1, chunks + 1):

            @pl.when(used == n)
            def _():
                for c in range(n):
                    kv_copy(r, 0, c).wait()
                sc[r, :, : n * ch] = lax.dot_general(
                    qbd[r], kv[r, 0, : n * ch, :], NT, preferred_element_type=F32
                )

        return carry

    lax.fori_loop(0, rows, score_step, 0)

    pos = iota((ROWS, length), 1)
    rest = []
    vf32 = vf.astype(F32)
    for r in range(rows):
        slot = lax.rem(lens[r] - SINKS, length)
        is_fresh = pos == slot
        s = jnp.where(is_fresh, fresh_scores[r], sc[r]) / math.sqrt(HD)
        s = jnp.where(pos < live_of(r), s, -jnp.inf)
        ss = sink_s[r]
        top = jnp.maximum(
            jnp.max(s, axis=-1, keepdims=True), jnp.max(ss, axis=-1, keepdims=True)
        )
        e = jnp.exp(s - top)
        es = jnp.exp(ss - top)
        tot = jnp.sum(e, axis=-1, keepdims=True) + jnp.sum(es, axis=-1, keepdims=True)
        w = (e / tot).astype(BF).astype(F32)
        fresh_w = jnp.sum(jnp.where(is_fresh, w, 0.0), axis=-1, keepdims=True)
        rest.append(fresh_w * vf32[r : r + 1, :] + dot((es / tot).astype(BF), sink[r, 1]))
        wts[r] = jnp.where(is_fresh, 0.0, w).astype(BF)

    def value_step(r, carry):
        used = (live_of(r) + ch - 1) // ch
        for n in range(1, chunks + 1):

            @pl.when(used == n)
            def _():
                for c in range(n):
                    kv_copy(r, 1, c).wait()
                acc[r] = dot(wts[r, :, : n * ch], kv[r, 1, : n * ch, :])

        return carry

    lax.fori_loop(0, rows, value_step, 0)

    attended = [
        jnp.sum(jnp.where(head_mask, acc[r] + rest[r], 0.0), axis=0, keepdims=True)
        for r in range(rows)
    ]
    attended = jnp.concatenate(attended, axis=0).astype(BF)
    ow_copy.wait()
    mine = dot(attended, ow_buf[...])
    part[...] = mine
    part_low[...] = mine.astype(BF)


def attend(groups, heads_axis, freq, lens, hidden, gain, bias, sink, idx, rw, w, win, ow):
    rows, width = hidden.shape
    local = bias.shape[1]
    length = win.shape[2]
    chunks = 4 if length % 4 == 0 else 1
    span = rows + CAP * groups
    return pl.pallas_call(
        functools.partial(attend_kernel, groups, heads_axis),
        out_shape=(
            jax.ShapeDtypeStruct((rows, width), F32),
            jax.ShapeDtypeStruct((rows, width), BF),
            jax.ShapeDtypeStruct((rows, 2, local), BF),
            jax.ShapeDtypeStruct((groups * span, groups * rows), BF),
            jax.ShapeDtypeStruct((groups * rows, width // groups), BF),
        ),
        in_specs=[VM] + [HB] * 10,
        out_specs=(VM,) * 5,
        scratch_shapes=[
            pltpu.SMEM(lens.shape, lens.dtype),
            pltpu.VMEM(hidden.shape, hidden.dtype),
            pltpu.VMEM(gain.shape, gain.dtype),
            pltpu.VMEM(bias.shape, bias.dtype),
            pltpu.VMEM(sink.shape, sink.dtype),
            pltpu.VMEM(idx.shape, idx.dtype),
            pltpu.VMEM(rw.shape, rw.dtype),
            pltpu.VMEM((3, width, local), BF),
            pltpu.VMEM((rows, 2, length, local), BF),
            pltpu.VMEM((local, width), BF),
            pltpu.VMEM((rows, ROWS, local), BF),
            pltpu.VMEM((rows, ROWS, length), F32),
            pltpu.VMEM((rows, ROWS, length), BF),
            pltpu.VMEM((rows, ROWS, local), F32),
            pltpu.SemaphoreType.DMA((7,)),
            pltpu.SemaphoreType.DMA((3, 2)),
            pltpu.SemaphoreType.DMA((rows, 2, chunks)),
            pltpu.SemaphoreType.DMA(()),
        ],
        compiler_params=params(52 * MB),
        name="attend",
    )(freq, *map(stay, (lens, hidden, gain, bias, sink, idx, rw, w, win, ow)))


def dispatch_kernel(groups, others, mine, hidden, gain, gate_vec, big, meta, *rest):
    parts, (send, own_out, keep) = rest[:others], rest[others:]
    rows, width = hidden.shape
    summed = mine[...]
    for p in parts:
        summed = summed + p[...].astype(F32)
    resid = hidden[...].astype(F32) + summed
    keep[...] = resid
    ms = jnp.mean(resid * resid, axis=-1, keepdims=True)
    tokens = (resid * lax.rsqrt(ms + EPSILON) * gain[...]).astype(BF).astype(F32)
    gate = jax.nn.sigmoid(jnp.sum(tokens * gate_vec[...], axis=-1, keepdims=True))
    w = width // groups
    stacked = jnp.concatenate([tokens[:, j * w : (j + 1) * w] for j in range(groups)], axis=0)
    placed = dot(big[...], stacked.astype(BF)).astype(BF)
    lane = iota((rows, w), 1)
    extra = jnp.zeros((rows, w), F32)
    for p, term in enumerate(split3(gate)):
        extra = extra + jnp.where(lane == 3 * CAP + p, term, 0.0)
    span = placed.shape[0] // groups
    full = send.shape[0] // groups
    for g in range(groups):
        send[g * full : g * full + span, :] = placed[g * span : (g + 1) * span, :]
        told = meta[g * rows : (g + 1) * rows, :].astype(F32) + extra
        send[g * full + span : (g + 1) * full, :] = told.astype(BF)
    slot = own_out.shape[1]
    start = pl.multiple_of(lax.axis_index("head") * slot, HD)
    own_out[...] = keep[:, pl.ds(start, slot)]


def dispatch(groups, slot, mine, parts, hidden, gain, gate_vec, big, meta):
    rows, width = hidden.shape
    return pl.pallas_call(
        functools.partial(dispatch_kernel, groups, len(parts)),
        out_shape=(
            jax.ShapeDtypeStruct((big.shape[0] + groups * rows, width // groups), BF),
            jax.ShapeDtypeStruct((rows, slot), F32),
        ),
        in_specs=[VM] * (6 + len(parts)),
        out_specs=(VM,) * 2,
        scratch_shapes=[pltpu.VMEM((rows, width), F32)],
        compiler_params=params(16 * MB),
        name="dispatch",
    )(mine, hidden, gain, gate_vec, big, meta, *parts)


def shared_in_kernel(groups, rows, arrived, weights, out, buf, sem):
    span = arrived.shape[0] // groups
    x = jnp.concatenate(
        [arrived[g * span : g * span + rows, :] for g in range(groups)], axis=0
    )
    tokens = x.shape[0]
    copies = []
    for i, first in enumerate(range(0, weights.shape[2], SPAN)):
        at = slice(first, min(first + SPAN, weights.shape[2]))
        both = jnp.concatenate([dot(x, weights[0, :, at]), dot(x, weights[1, :, at])], axis=0)
        buf[at, :] = both.T.astype(BF)
        copies.append(pltpu.make_async_copy(buf.at[at], out.at[at], sem.at[i]))
        copies[-1].start()
    for copy in copies:
        copy.wait()


def shared_in(groups, rows, arrived, weights):
    shape = (weights.shape[2], 2 * groups * rows)
    return pl.pallas_call(
        functools.partial(shared_in_kernel, groups, rows),
        out_shape=jax.ShapeDtypeStruct(shape, BF),
        in_specs=[VM] * 2,
        out_specs=HB,
        scratch_shapes=[
            pltpu.VMEM(shape, BF),
            pltpu.SemaphoreType.DMA((pl.cdiv(shape[0], SPAN),)),
        ],
        compiler_params=params(16 * MB),
        name="shared_in",
    )(arrived, weights)


def expert_kernel(groups, rows, arrived, gu_hbm, down_hbm, out, gu, down, gu_sem, down_sem):
    pieces = down_sem.shape[0]
    piece = down.shape[0] // pieces

    def gu_copy(t, i):
        at = pl.ds(i * piece, piece)
        return pltpu.make_async_copy(gu_hbm.at[t, at], gu.at[t, at], gu_sem.at[t, i])

    def down_copy(i):
        at = pl.ds(i * piece, piece)
        return pltpu.make_async_copy(down_hbm.at[at], down.at[at], down_sem.at[i])

    for i in range(pieces):
        gu_copy(0, i).start()
        gu_copy(1, i).start()
    for i in range(pieces):
        down_copy(i).start()

    slots = groups * CAP
    total = arrived.shape[0]
    span = total // groups
    line, lane = iota((groups * slots, total), 0), iota((groups * slots, total), 1)
    j, g, c = line // slots, line % slots // CAP, line % CAP
    pickm = one(lane == g * span + rows + j * CAP + c).astype(BF)
    x = dot(pickm, arrived[...])
    x = jnp.concatenate(
        [x[jj * slots : (jj + 1) * slots, :] for jj in range(groups)], axis=1
    ).astype(BF)
    hidden = []
    for i in range(pieces):
        at = slice(i * piece, (i + 1) * piece)
        gu_copy(0, i).wait()
        gate = lax.dot_general(x, gu[0, at, :], NT, preferred_element_type=F32)
        gu_copy(1, i).wait()
        up = lax.dot_general(x, gu[1, at, :], NT, preferred_element_type=F32)
        hidden.append((jax.nn.silu(gate) * up).astype(BF))
    result = jnp.zeros((slots, down.shape[1]), F32)
    for i in range(pieces):
        down_copy(i).wait()
        result = result + dot(hidden[i], down[i * piece : (i + 1) * piece, :])
    out[...] = result


def experts(groups, rows, arrived, gate_up, down):
    fe, width = down.shape
    pieces = fe // 352 if fe % 352 == 0 else 1
    slots = groups * CAP
    return pl.pallas_call(
        functools.partial(expert_kernel, groups, rows),
        out_shape=jax.ShapeDtypeStruct((slots, width), F32),
        in_specs=[VM, HB, HB],
        out_specs=VM,
        scratch_shapes=[
            pltpu.VMEM(gate_up.shape, BF),
            pltpu.VMEM(down.shape, BF),
            pltpu.SemaphoreType.DMA((2, pieces)),
            pltpu.SemaphoreType.DMA((pieces,)),
        ],
        compiler_params=params(32 * MB),
        cost_estimate=pl.CostEstimate(
            flops=6 * slots * fe * width, transcendentals=slots * fe, bytes_accessed=6 * fe * width
        ),
        name="experts",
    )(arrived, stay(gate_up), stay(down))


def give_back_kernel(groups, heads_axis, rows, sums, down, routed, arrived, out):
    total = sums[0].astype(F32)
    for g in range(1, groups):
        total = total + sums[g].astype(F32)
    tokens = groups * rows
    hidden = jax.nn.silu(total) * pltpu.roll(total, tokens, 1)
    hidden = hidden[:, :tokens].T.astype(BF)
    span = arrived.shape[0] // groups
    told = jnp.concatenate(
        [arrived[(g + 1) * span - rows : (g + 1) * span, :HD] for g in range(groups)], axis=0
    ).astype(F32)

    def column(k):
        return told[:, 3 * k : 3 * k + 1] + told[:, 3 * k + 1 : 3 * k + 2] + told[:, 3 * k + 2 : 3 * k + 3]

    gate = column(CAP)
    weight = [column(c) for c in range(CAP)]
    w = down.shape[2]
    ratio = groups // heads_axis
    for j in range(groups):
        shared = gate * dot(hidden, down[j])
        h, half = j // ratio, j % ratio
        for g in range(groups):
            at = slice(g * rows, (g + 1) * rows)
            value = shared[at]
            for c in range(CAP):
                line = routed[g * CAP + c : g * CAP + c + 1, j * w : (j + 1) * w]
                value = value + weight[c][at] * line
            to = (g * heads_axis + h) * rows
            out[to : to + rows, half * w : (half + 1) * w] = value.astype(BF)


def give_back(groups, heads_axis, rows, sums, down, routed, arrived):
    return pl.pallas_call(
        functools.partial(give_back_kernel, groups, heads_axis, rows),
        out_shape=jax.ShapeDtypeStruct(
            (groups * heads_axis * rows, routed.shape[1] // heads_axis), BF
        ),
        in_specs=[VM] * 4,
        out_specs=VM,
        compiler_params=params(16 * MB),
        name="give_back",
    )(sums, down, routed, arrived)


def finish_kernel(returned, own, out):
    rows = own.shape[0]
    total = own[...]
    for i in range(returned.shape[0] // rows):
        total = total + returned[i * rows : (i + 1) * rows, :].astype(F32)
    out[...] = total.astype(BF)


def finish(returned, own):
    return pl.pallas_call(
        finish_kernel,
        out_shape=jax.ShapeDtypeStruct(own.shape, BF),
        in_specs=[VM] * 2,
        out_specs=VM,
        compiler_params=params(16 * MB),
        name="finish",
    )(returned, own)


def local(
    hidden_state,
    attend_gain,
    input_weight,
    input_bias,
    output_weight,
    window_cache,
    sink_cache,
    lengths,
    expert_index,
    router_weight,
    mixture_gain,
    expert_gate_up,
    expert_down,
    shared_gate_up,
    shared_down,
    shared_gate,
):
    rows, width = hidden_state.shape
    local_width = input_weight.shape[2]
    groups = lax.axis_size("req")
    heads_axis = lax.axis_size("head")
    slot = width // heads_axis
    half = HD // 2
    frequencies = F32(ROPE_BASE) ** (-(2.0 / HD) * jnp.arange(half).astype(F32))
    down = shared_down.reshape(groups, shared_down.shape[0] // groups, shared_down.shape[1])
    down = lax.all_to_all(down, "req", split_axis=0, concat_axis=0, tiled=True)

    part, low, new_kv, big, meta = attend(
        groups,
        heads_axis,
        frequencies[None],
        lengths,
        hidden_state,
        attend_gain[None],
        input_bias,
        sink_cache,
        expert_index.T,
        router_weight.T,
        jnp.transpose(input_weight, (1, 0, 2)),
        window_cache,
        output_weight,
    )
    parts = [
        lax.ppermute(part if k == 1 else low, "head", [(j, j ^ k) for j in range(heads_axis)])
        for k in range(1, heads_axis)
    ]
    parts, down = lax.optimization_barrier((parts, down))
    send, own = dispatch(
        groups, slot, part, parts, hidden_state, mixture_gain[None], shared_gate[None], big, meta
    )
    arrived = lax.all_to_all(send, "req", split_axis=0, concat_axis=0, tiled=True)
    sums = shared_in(groups, rows, arrived, shared_gate_up)
    sums = sums.reshape(groups, sums.shape[0] // groups, sums.shape[1])
    sums = lax.all_to_all(sums, "req", split_axis=0, concat_axis=0, tiled=True)
    routed = experts(groups, rows, arrived, expert_gate_up, expert_down)
    back = give_back(groups, heads_axis, rows, sums, down, routed, arrived)
    returned = lax.all_to_all(back, ("req", "head"), split_axis=0, concat_axis=0, tiled=True)
    return finish(returned, own), new_kv


def solution(mesh):
    return jax.shard_map(
        local,
        mesh=mesh,
        in_specs=(
            P("req", None),
            P(),
            P(None, None, "head"),
            P(None, "head"),
            P("head", None),
            P("req", None, None, "head"),
            P("req", None, None, "head"),
            P("req"),
            P("req", None),
            P("req", None),
            P(),
            P(None, ("req", "head"), None),
            P(("req", "head"), None),
            P(None, "req", "head"),
            P("head", "req"),
            P(),
        ),
        out_specs=(P("req", "head"), P("req", None, "head")),
        check_vma=False,
    )
```

```python
import functools
import math

import jax
import jax.numpy as jnp
from jax import lax
from jax.experimental import pallas as pl
from jax.experimental.pallas import tpu as pltpu
from jax.sharding import PartitionSpec as P

HD = 128
EXPERTS = 32
FE = 1408
SINKS = 4
CAP = 2
ROWS = 8

EPSILON = 1e-06
ROPE_BASE = 1000000.0
MB = 1 << 20
BF = jnp.bfloat16
F32 = jnp.float32


def stay(x):
    return pltpu.with_memory_space_constraint(x, pltpu.HBM)


NT = (((1,), (1,)), ((), ()))


def iota(shape, dim):
    return lax.broadcasted_iota(jnp.int32, shape, dim)


def one(cond):
    return jnp.where(cond, 1.0, 0.0).astype(F32)


def dot(a, b):
    return jnp.dot(a, b, preferred_element_type=F32)


def split3(x):
    hi = x.astype(BF).astype(F32)
    mid = (x - hi).astype(BF).astype(F32)
    lo = (x - hi - mid).astype(BF).astype(F32)
    return hi, mid, lo


def params(limit, **kw):
    return pltpu.CompilerParams(vmem_limit_bytes=limit, **kw)


VM = pl.BlockSpec(memory_space=pltpu.VMEM)
SM = pl.BlockSpec(memory_space=pltpu.SMEM)
HB = pl.BlockSpec(memory_space=pltpu.HBM)


def routing_tables(groups, heads_axis, idx, rw, big_out, meta_out):
    rows = idx.shape[1]
    local_experts = EXPERTS // groups
    pick = lax.axis_index("head") // (heads_axis // local_experts)
    hit = jnp.zeros((EXPERTS, rows), F32)
    comb = jnp.zeros((EXPERTS, rows), F32)
    line_e = iota((EXPERTS, rows), 0)
    for k in range(idx.shape[0]):
        eq = one(idx[k : k + 1, :] == line_e)
        hit = hit + eq
        comb = comb + eq * rw[k : k + 1, :]
    above = one(iota((rows, rows), 0) < iota((rows, rows), 1))
    rank = dot(hit.astype(BF), above.astype(BF))
    sel = [hit * one(rank == c) for c in range(CAP)]
    span = rows + CAP * groups
    total = groups * span
    row_g = iota((total, EXPERTS), 0) // span
    row_t = iota((total, EXPERTS), 0) % span
    mine = iota((total, EXPERTS), 1) == row_g * local_experts + pick
    z = jnp.zeros((total, rows), F32)
    for c in range(CAP):
        pickc = mine & (row_t >= rows) & ((row_t - rows) % CAP == c)
        z = z + dot(one(pickc).astype(BF), sel[c].astype(BF))
    nb = groups * rows
    rep = one(iota((rows, nb), 0) == iota((rows, nb), 1) % rows)
    zz = dot(z.astype(BF), rep.astype(BF))
    g2 = iota((total, nb), 0) // span
    t2 = iota((total, nb), 0) % span
    j2 = iota((total, nb), 1) // rows
    r2 = iota((total, nb), 1) % rows
    direct = one((j2 == g2) & (r2 == t2))
    placed = zz * one(j2 == (t2 - rows) // CAP)
    big_out[...] = jnp.where(t2 < rows, direct, placed).astype(BF)

    w = meta_out.shape[1]
    again = one(iota((nb, rows), 0) % rows == iota((nb, rows), 1)).astype(BF)
    keep = iota((nb, EXPERTS), 1) == (iota((nb, EXPERTS), 0) // rows) * local_experts + pick
    meta = jnp.zeros((nb, w), F32)
    for c in range(CAP):
        for p, term in enumerate(split3(comb * sel[c])):
            wide = lax.dot_general(again, term.astype(BF), NT, preferred_element_type=F32)
            wide = jnp.where(keep, wide, 0.0).astype(BF)
            column = one(iota((EXPERTS, w), 1) == 3 * c + p).astype(BF)
            meta = meta + dot(wide, column)
    meta_out[...] = meta.astype(BF)


def attend_kernel(
    groups,
    heads_axis,
    freq,
    lens_hbm,
    hidden_hbm,
    gain_hbm,
    bias_hbm,
    sink_hbm,
    idx_hbm,
    rw_hbm,
    w_hbm,
    win_hbm,
    ow_hbm,
    part,
    part_low,
    new_kv,
    big_out,
    meta_out,
    lens,
    hidden,
    gain,
    bias,
    sink,
    idx,
    rw,
    w_buf,
    kv,
    ow_buf,
    qbd,
    sc,
    wts,
    acc,
    small_sem,
    w_sem,
    kv_sem,
    ow_sem,
):
    rows, width = hidden.shape
    local = bias.shape[1]
    length = kv.shape[2]
    chunks = kv_sem.shape[2]
    ch = length // chunks
    halves = w_sem.shape[1]
    wc = width // halves

    small = [
        pltpu.make_async_copy(src, dst, small_sem.at[i])
        for i, (src, dst) in enumerate(
            (
                (lens_hbm, lens),
                (hidden_hbm, hidden),
                (gain_hbm, gain),
                (bias_hbm, bias),
                (idx_hbm, idx),
                (rw_hbm, rw),
                (sink_hbm, sink),
            )
        )
    ]

    def w_copy(c, i):
        return pltpu.make_async_copy(
            w_hbm.at[c, pl.ds(i * wc, wc)], w_buf.at[c, pl.ds(i * wc, wc)], w_sem.at[c, i]
        )

    def kv_copy(r, t, c):
        return pltpu.make_async_copy(
            win_hbm.at[r, t, pl.ds(c * ch, ch)], kv.at[r, t, pl.ds(c * ch, ch)], kv_sem.at[r, t, c]
        )

    def live_of(r):
        return jnp.minimum(lens[r] - SINKS + 1, length)

    def fetch(t):
        def step(r, carry):
            live = live_of(r)
            for c in range(chunks):

                @pl.when(c * ch < live)
                def _():
                    kv_copy(r, t, c).start()

            return carry

        lax.fori_loop(0, rows, step, 0)

    for copy in small:
        copy.start()
    for c in range(3):
        for i in range(halves):
            w_copy(c, i).start()
    small[0].wait()
    fetch(0)
    fetch(1)
    ow_copy = pltpu.make_async_copy(ow_hbm, ow_buf, ow_sem)
    ow_copy.start()
    for copy in small[1:]:
        copy.wait()

    routing_tables(groups, heads_axis, idx, rw, big_out, meta_out)

    place = jnp.concatenate([jnp.full((1, HD // 2), lens[r], jnp.int32) for r in range(rows)], axis=0)
    angles = place.astype(F32) * freq[...]
    cosine, sine = jnp.cos(angles), jnp.sin(angles)
    cos = jnp.concatenate([cosine, cosine], axis=1)
    sin = jnp.concatenate([-sine, sine], axis=1)

    x = hidden[...].astype(F32)
    ms = jnp.mean(x * x, axis=-1, keepdims=True)
    normed = (x * lax.rsqrt(ms + EPSILON) * gain[...]).astype(BF)
    proj = []
    for c in range(3):
        total_c = bias[c : c + 1, :]
        for i in range(halves):
            w_copy(c, i).wait()
            total_c = total_c + dot(
                normed[:, i * wc : (i + 1) * wc], w_buf[c, i * wc : (i + 1) * wc, :]
            )
        proj.append(total_c)

    def rotate(v):
        outs = []
        for h in range(local // HD):
            part_h = v[:, h * HD : (h + 1) * HD]
            outs.append(part_h * cos + pltpu.roll(part_h, HD // 2, 1) * sin)
        return jnp.concatenate(outs, axis=1)

    q = rotate(proj[0]).astype(BF).astype(F32)
    kf = rotate(proj[1]).astype(BF)
    vf = proj[2].astype(BF)
    new_kv[...] = jnp.stack([kf.astype(F32), vf.astype(F32)], axis=1).astype(BF)
    head_mask = iota((ROWS, local), 1) // HD == iota((ROWS, local), 0)
    q3 = jnp.where(head_mask[None], q[:, None, :], 0.0)
    qbd[...] = q3.astype(BF)
    fresh_scores = jnp.sum(q3 * kf.astype(F32)[:, None, :], axis=-1, keepdims=True)

    sink_s = [
        lax.dot_general(qbd[r], sink[r, 0], NT, preferred_element_type=F32) / math.sqrt(HD)
        for r in range(rows)
    ]

    def score_step(r, carry):
        used = (live_of(r) + ch - 1) // ch
        for n in range(1, chunks + 1):

            @pl.when(used == n)
            def _():
                for c in range(n):
                    kv_copy(r, 0, c).wait()
                sc[r, :, : n * ch] = lax.dot_general(
                    qbd[r], kv[r, 0, : n * ch, :], NT, preferred_element_type=F32
                )

        return carry

    lax.fori_loop(0, rows, score_step, 0)

    pos = iota((ROWS, length), 1)
    rest = []
    vf32 = vf.astype(F32)
    for r in range(rows):
        slot = lax.rem(lens[r] - SINKS, length)
        is_fresh = pos == slot
        s = jnp.where(is_fresh, fresh_scores[r], sc[r]) / math.sqrt(HD)
        s = jnp.where(pos < live_of(r), s, -jnp.inf)
        ss = sink_s[r]
        top = jnp.maximum(
            jnp.max(s, axis=-1, keepdims=True), jnp.max(ss, axis=-1, keepdims=True)
        )
        e = jnp.exp(s - top)
        es = jnp.exp(ss - top)
        tot = jnp.sum(e, axis=-1, keepdims=True) + jnp.sum(es, axis=-1, keepdims=True)
        w = (e / tot).astype(BF).astype(F32)
        fresh_w = jnp.sum(jnp.where(is_fresh, w, 0.0), axis=-1, keepdims=True)
        rest.append(fresh_w * vf32[r : r + 1, :] + dot((es / tot).astype(BF), sink[r, 1]))
        wts[r] = jnp.where(is_fresh, 0.0, w).astype(BF)

    def value_step(r, carry):
        used = (live_of(r) + ch - 1) // ch
        for n in range(1, chunks + 1):

            @pl.when(used == n)
            def _():
                for c in range(n):
                    kv_copy(r, 1, c).wait()
                acc[r] = dot(wts[r, :, : n * ch], kv[r, 1, : n * ch, :])

        return carry

    lax.fori_loop(0, rows, value_step, 0)

    attended = [
        jnp.sum(jnp.where(head_mask, acc[r] + rest[r], 0.0), axis=0, keepdims=True)
        for r in range(rows)
    ]
    attended = jnp.concatenate(attended, axis=0).astype(BF)
    ow_copy.wait()
    mine = dot(attended, ow_buf[...])
    part[...] = mine
    part_low[...] = mine.astype(BF)


def attend(groups, heads_axis, freq, lens, hidden, gain, bias, sink, idx, rw, w, win, ow):
    rows, width = hidden.shape
    local = bias.shape[1]
    length = win.shape[2]
    chunks = 4 if length % 4 == 0 else 1
    span = rows + CAP * groups
    return pl.pallas_call(
        functools.partial(attend_kernel, groups, heads_axis),
        out_shape=(
            jax.ShapeDtypeStruct((rows, width), F32),
            jax.ShapeDtypeStruct((rows, width), BF),
            jax.ShapeDtypeStruct((rows, 2, local), BF),
            jax.ShapeDtypeStruct((groups * span, groups * rows), BF),
            jax.ShapeDtypeStruct((groups * rows, 2 * groups * rows), BF),
        ),
        in_specs=[VM] + [HB] * 10,
        out_specs=(VM,) * 5,
        scratch_shapes=[
            pltpu.SMEM(lens.shape, lens.dtype),
            pltpu.VMEM(hidden.shape, hidden.dtype),
            pltpu.VMEM(gain.shape, gain.dtype),
            pltpu.VMEM(bias.shape, bias.dtype),
            pltpu.VMEM(sink.shape, sink.dtype),
            pltpu.VMEM(idx.shape, idx.dtype),
            pltpu.VMEM(rw.shape, rw.dtype),
            pltpu.VMEM((3, width, local), BF),
            pltpu.VMEM((rows, 2, length, local), BF),
            pltpu.VMEM((local, width), BF),
            pltpu.VMEM((rows, ROWS, local), BF),
            pltpu.VMEM((rows, ROWS, length), F32),
            pltpu.VMEM((rows, ROWS, length), BF),
            pltpu.VMEM((rows, ROWS, local), F32),
            pltpu.SemaphoreType.DMA((7,)),
            pltpu.SemaphoreType.DMA((3, 2)),
            pltpu.SemaphoreType.DMA((rows, 2, chunks)),
            pltpu.SemaphoreType.DMA(()),
        ],
        compiler_params=params(52 * MB),
        name="attend",
    )(freq, *map(stay, (lens, hidden, gain, bias, sink, idx, rw, w, win, ow)))


def dispatch_kernel(groups, others, mine, hidden, gain, gate_vec, big, meta, *rest):
    parts, (send, meta_out, own_out, keep) = rest[:others], rest[others:]
    rows, width = hidden.shape
    summed = mine[...]
    for p in parts:
        summed = summed + p[...].astype(F32)
    resid = hidden[...].astype(F32) + summed
    keep[...] = resid
    ms = jnp.mean(resid * resid, axis=-1, keepdims=True)
    tokens = (resid * lax.rsqrt(ms + EPSILON) * gain[...]).astype(BF).astype(F32)
    gate = jax.nn.sigmoid(jnp.sum(tokens * gate_vec[...], axis=-1, keepdims=True))
    w = width // groups
    stacked = jnp.concatenate([tokens[:, j * w : (j + 1) * w] for j in range(groups)], axis=0)
    placed = dot(big[...], stacked.astype(BF)).astype(BF)
    lane = iota((rows, meta.shape[1]), 1)
    extra = jnp.zeros((rows, meta.shape[1]), F32)
    for p, term in enumerate(split3(gate)):
        extra = extra + jnp.where(lane == 3 * CAP + p, term, 0.0)
    send[...] = placed
    for g in range(groups):
        at = slice(g * rows, (g + 1) * rows)
        meta_out[at, :] = (meta[at, :].astype(F32) + extra).astype(BF)
    slot = own_out.shape[1]
    start = pl.multiple_of(lax.axis_index("head") * slot, HD)
    own_out[...] = keep[:, pl.ds(start, slot)]


def dispatch(groups, slot, mine, parts, hidden, gain, gate_vec, big, meta):
    rows, width = hidden.shape
    return pl.pallas_call(
        functools.partial(dispatch_kernel, groups, len(parts)),
        out_shape=(
            jax.ShapeDtypeStruct((big.shape[0], width // groups), BF),
            jax.ShapeDtypeStruct(meta.shape, BF),
            jax.ShapeDtypeStruct((rows, slot), F32),
        ),
        in_specs=[VM] * (6 + len(parts)),
        out_specs=(VM,) * 3,
        scratch_shapes=[pltpu.VMEM((rows, width), F32)],
        compiler_params=params(16 * MB),
        name="dispatch",
    )(mine, hidden, gain, gate_vec, big, meta, *parts)


def shared_in_kernel(groups, rows, arrived, weights, meta, out):
    span = arrived.shape[0] // groups
    x = jnp.concatenate(
        [arrived[g * span : g * span + rows, :] for g in range(groups)], axis=0
    )
    both = jnp.concatenate([dot(x, weights[0]), dot(x, weights[1])], axis=0).T
    piece = both.shape[0] // groups
    for g in range(groups):
        out[g, :piece, :] = both[g * piece : (g + 1) * piece, :].astype(BF)
        out[g, piece:, :] = meta[g * rows : (g + 1) * rows, :]


def shared_in(groups, rows, arrived, weights, meta):
    piece = weights.shape[2] // groups
    return pl.pallas_call(
        functools.partial(shared_in_kernel, groups, rows),
        out_shape=jax.ShapeDtypeStruct((groups, piece + rows, 2 * groups * rows), BF),
        in_specs=[VM] * 3,
        out_specs=VM,
        compiler_params=params(16 * MB),
        name="shared_in",
    )(arrived, weights, meta)


def expert_kernel(groups, rows, arrived, gu_hbm, down_hbm, out, gu, down, gu_sem, down_sem):
    pieces = down_sem.shape[0]
    piece = down.shape[0] // pieces

    def gu_copy(t, i):
        at = pl.ds(i * piece, piece)
        return pltpu.make_async_copy(gu_hbm.at[t, at], gu.at[t, at], gu_sem.at[t, i])

    def down_copy(i):
        at = pl.ds(i * piece, piece)
        return pltpu.make_async_copy(down_hbm.at[at], down.at[at], down_sem.at[i])

    for i in range(pieces):
        gu_copy(0, i).start()
        gu_copy(1, i).start()
    for i in range(pieces):
        down_copy(i).start()

    slots = groups * CAP
    total = arrived.shape[0]
    span = total // groups
    line, lane = iota((groups * slots, total), 0), iota((groups * slots, total), 1)
    j, g, c = line // slots, line % slots // CAP, line % CAP
    pickm = one(lane == g * span + rows + j * CAP + c).astype(BF)
    x = dot(pickm, arrived[...])
    x = jnp.concatenate(
        [x[jj * slots : (jj + 1) * slots, :] for jj in range(groups)], axis=1
    ).astype(BF)
    hidden = []
    for i in range(pieces):
        at = slice(i * piece, (i + 1) * piece)
        gu_copy(0, i).wait()
        gate = lax.dot_general(x, gu[0, at, :], NT, preferred_element_type=F32)
        gu_copy(1, i).wait()
        up = lax.dot_general(x, gu[1, at, :], NT, preferred_element_type=F32)
        hidden.append((jax.nn.silu(gate) * up).astype(BF))
    result = jnp.zeros((slots, down.shape[1]), F32)
    for i in range(pieces):
        down_copy(i).wait()
        result = result + dot(hidden[i], down[i * piece : (i + 1) * piece, :])
    out[...] = result


def experts(groups, rows, arrived, gate_up, down):
    fe, width = down.shape
    pieces = fe // 352 if fe % 352 == 0 else 1
    slots = groups * CAP
    return pl.pallas_call(
        functools.partial(expert_kernel, groups, rows),
        out_shape=jax.ShapeDtypeStruct((slots, width), F32),
        in_specs=[VM, HB, HB],
        out_specs=VM,
        scratch_shapes=[
            pltpu.VMEM(gate_up.shape, BF),
            pltpu.VMEM(down.shape, BF),
            pltpu.SemaphoreType.DMA((2, pieces)),
            pltpu.SemaphoreType.DMA((pieces,)),
        ],
        compiler_params=params(32 * MB),
        cost_estimate=pl.CostEstimate(
            flops=6 * slots * fe * width, transcendentals=slots * fe, bytes_accessed=6 * fe * width
        ),
        name="experts",
    )(arrived, stay(gate_up), stay(down))


def give_back_kernel(groups, heads_axis, rows, sums, down, routed, out):
    piece = down.shape[1]
    total = sums[0, :piece, :].astype(F32)
    for g in range(1, groups):
        total = total + sums[g, :piece, :].astype(F32)
    tokens = groups * rows
    hidden = jax.nn.silu(total) * pltpu.roll(total, tokens, 1)
    hidden = hidden[:, :tokens].T.astype(BF)
    told = jnp.concatenate(
        [sums[g, piece:, :].astype(F32)[:, :HD] for g in range(groups)], axis=0
    )

    def column(k):
        return told[:, 3 * k : 3 * k + 1] + told[:, 3 * k + 1 : 3 * k + 2] + told[:, 3 * k + 2 : 3 * k + 3]

    gate = column(CAP)
    weight = [column(c) for c in range(CAP)]
    w = down.shape[2]
    ratio = groups // heads_axis
    for j in range(groups):
        shared = gate * dot(hidden, down[j])
        h, half = j // ratio, j % ratio
        for g in range(groups):
            at = slice(g * rows, (g + 1) * rows)
            value = shared[at]
            for c in range(CAP):
                line = routed[g * CAP + c : g * CAP + c + 1, j * w : (j + 1) * w]
                value = value + weight[c][at] * line
            to = (g * heads_axis + h) * rows
            out[to : to + rows, half * w : (half + 1) * w] = value.astype(BF)


def give_back(groups, heads_axis, rows, sums, down, routed):
    return pl.pallas_call(
        functools.partial(give_back_kernel, groups, heads_axis, rows),
        out_shape=jax.ShapeDtypeStruct(
            (groups * heads_axis * rows, routed.shape[1] // heads_axis), BF
        ),
        in_specs=[VM] * 3,
        out_specs=VM,
        compiler_params=params(16 * MB),
        name="give_back",
    )(sums, down, routed)


def finish_kernel(returned, own, out):
    rows = own.shape[0]
    total = own[...]
    for i in range(returned.shape[0] // rows):
        total = total + returned[i * rows : (i + 1) * rows, :].astype(F32)
    out[...] = total.astype(BF)


def finish(returned, own):
    return pl.pallas_call(
        finish_kernel,
        out_shape=jax.ShapeDtypeStruct(own.shape, BF),
        in_specs=[VM] * 2,
        out_specs=VM,
        compiler_params=params(16 * MB),
        name="finish",
    )(returned, own)


def local(
    hidden_state,
    attend_gain,
    input_weight,
    input_bias,
    output_weight,
    window_cache,
    sink_cache,
    lengths,
    expert_index,
    router_weight,
    mixture_gain,
    expert_gate_up,
    expert_down,
    shared_gate_up,
    shared_down,
    shared_gate,
):
    rows, width = hidden_state.shape
    local_width = input_weight.shape[2]
    groups = lax.axis_size("req")
    heads_axis = lax.axis_size("head")
    slot = width // heads_axis
    half = HD // 2
    frequencies = F32(ROPE_BASE) ** (-(2.0 / HD) * jnp.arange(half).astype(F32))
    down = shared_down.reshape(groups, shared_down.shape[0] // groups, shared_down.shape[1])
    down = lax.all_to_all(down, "req", split_axis=0, concat_axis=0, tiled=True)

    part, low, new_kv, big, meta = attend(
        groups,
        heads_axis,
        frequencies[None],
        lengths,
        hidden_state,
        attend_gain[None],
        input_bias,
        sink_cache,
        expert_index.T,
        router_weight.T,
        jnp.transpose(input_weight, (1, 0, 2)),
        window_cache,
        output_weight,
    )
    parts = [
        lax.ppermute(part if k == 1 else low, "head", [(j, j ^ k) for j in range(heads_axis)])
        for k in range(1, heads_axis)
    ]
    parts, down = lax.optimization_barrier((parts, down))
    send, meta, own = dispatch(
        groups, slot, part, parts, hidden_state, mixture_gain[None], shared_gate[None], big, meta
    )
    arrived = lax.all_to_all(send, "req", split_axis=0, concat_axis=0, tiled=True)
    sums = shared_in(groups, rows, arrived, shared_gate_up, meta)
    sums = lax.all_to_all(sums, "req", split_axis=0, concat_axis=0, tiled=True)
    routed = experts(groups, rows, arrived, expert_gate_up, expert_down)
    back = give_back(groups, heads_axis, rows, sums, down, routed)
    returned = lax.all_to_all(back, ("req", "head"), split_axis=0, concat_axis=0, tiled=True)
    return finish(returned, own), new_kv


def solution(mesh):
    return jax.shard_map(
        local,
        mesh=mesh,
        in_specs=(
            P("req", None),
            P(),
            P(None, None, "head"),
            P(None, "head"),
            P("head", None),
            P("req", None, None, "head"),
            P("req", None, None, "head"),
            P("req"),
            P("req", None),
            P("req", None),
            P(),
            P(None, ("req", "head"), None),
            P(("req", "head"), None),
            P(None, "req", "head"),
            P("head", "req"),
            P(),
        ),
        out_specs=(P("req", "head"), P("req", None, "head")),
        check_vma=False,
    )
```

```python
import functools
import math

import jax
import jax.numpy as jnp
from jax import lax
from jax.experimental import pallas as pl
from jax.experimental.pallas import tpu as pltpu
from jax.sharding import PartitionSpec as P

HD = 128
EXPERTS = 32
FE = 1408
SINKS = 4
CAP = 2
ROWS = 8

EPSILON = 1e-06
ROPE_BASE = 1000000.0
MB = 1 << 20
SPAN = 384
BF = jnp.bfloat16
F32 = jnp.float32


def stay(x):
    return pltpu.with_memory_space_constraint(x, pltpu.HBM)


NT = (((1,), (1,)), ((), ()))


def iota(shape, dim):
    return lax.broadcasted_iota(jnp.int32, shape, dim)


def one(cond):
    return jnp.where(cond, 1.0, 0.0).astype(F32)


def dot(a, b):
    return jnp.dot(a, b, preferred_element_type=F32)


def split3(x):
    hi = x.astype(BF).astype(F32)
    mid = (x - hi).astype(BF).astype(F32)
    lo = (x - hi - mid).astype(BF).astype(F32)
    return hi, mid, lo


def params(limit, **kw):
    return pltpu.CompilerParams(vmem_limit_bytes=limit, **kw)


VM = pl.BlockSpec(memory_space=pltpu.VMEM)
SM = pl.BlockSpec(memory_space=pltpu.SMEM)
HB = pl.BlockSpec(memory_space=pltpu.HBM)


def routing_tables(groups, heads_axis, idx, rw, big_out, meta_out):
    rows = idx.shape[1]
    local_experts = EXPERTS // groups
    pick = lax.axis_index("head") // (heads_axis // local_experts)
    hit = jnp.zeros((EXPERTS, rows), F32)
    comb = jnp.zeros((EXPERTS, rows), F32)
    line_e = iota((EXPERTS, rows), 0)
    for k in range(idx.shape[0]):
        eq = one(idx[k : k + 1, :] == line_e)
        hit = hit + eq
        comb = comb + eq * rw[k : k + 1, :]
    above = one(iota((rows, rows), 0) < iota((rows, rows), 1))
    rank = dot(hit.astype(BF), above.astype(BF))
    sel = [hit * one(rank == c) for c in range(CAP)]
    span = rows + CAP * groups
    total = groups * span
    row_g = iota((total, EXPERTS), 0) // span
    row_t = iota((total, EXPERTS), 0) % span
    mine = iota((total, EXPERTS), 1) == row_g * local_experts + pick
    z = jnp.zeros((total, rows), F32)
    for c in range(CAP):
        pickc = mine & (row_t >= rows) & ((row_t - rows) % CAP == c)
        z = z + dot(one(pickc).astype(BF), sel[c].astype(BF))
    nb = groups * rows
    rep = one(iota((rows, nb), 0) == iota((rows, nb), 1) % rows)
    zz = dot(z.astype(BF), rep.astype(BF))
    g2 = iota((total, nb), 0) // span
    t2 = iota((total, nb), 0) % span
    j2 = iota((total, nb), 1) // rows
    r2 = iota((total, nb), 1) % rows
    direct = one((j2 == g2) & (r2 == t2))
    placed = zz * one(j2 == (t2 - rows) // CAP)
    big_out[...] = jnp.where(t2 < rows, direct, placed).astype(BF)

    w = meta_out.shape[1]
    again = one(iota((nb, rows), 0) % rows == iota((nb, rows), 1)).astype(BF)
    keep = iota((nb, EXPERTS), 1) == (iota((nb, EXPERTS), 0) // rows) * local_experts + pick
    meta = jnp.zeros((nb, w), F32)
    for c in range(CAP):
        for p, term in enumerate(split3(comb * sel[c])):
            wide = lax.dot_general(again, term.astype(BF), NT, preferred_element_type=F32)
            wide = jnp.where(keep, wide, 0.0).astype(BF)
            column = one(iota((EXPERTS, w), 1) == 3 * c + p).astype(BF)
            meta = meta + dot(wide, column)
    meta_out[...] = meta.astype(BF)


def attend_kernel(
    groups,
    heads_axis,
    freq,
    lens_hbm,
    hidden_hbm,
    gain_hbm,
    bias_hbm,
    sink_hbm,
    idx_hbm,
    rw_hbm,
    w_hbm,
    win_hbm,
    ow_hbm,
    part,
    part_low,
    new_kv,
    big_out,
    meta_out,
    lens,
    hidden,
    gain,
    bias,
    sink,
    idx,
    rw,
    w_buf,
    kv,
    ow_buf,
    qbd,
    sc,
    wts,
    acc,
    small_sem,
    w_sem,
    kv_sem,
    ow_sem,
):
    rows, width = hidden.shape
    local = bias.shape[1]
    length = kv.shape[2]
    chunks = kv_sem.shape[2]
    ch = length // chunks
    halves = w_sem.shape[1]
    wc = width // halves

    small = [
        pltpu.make_async_copy(src, dst, small_sem.at[i])
        for i, (src, dst) in enumerate(
            (
                (lens_hbm, lens),
                (hidden_hbm, hidden),
                (gain_hbm, gain),
                (bias_hbm, bias),
                (idx_hbm, idx),
                (rw_hbm, rw),
                (sink_hbm, sink),
            )
        )
    ]

    def w_copy(c, i):
        return pltpu.make_async_copy(
            w_hbm.at[c, pl.ds(i * wc, wc)], w_buf.at[c, pl.ds(i * wc, wc)], w_sem.at[c, i]
        )

    def kv_copy(r, t, c):
        return pltpu.make_async_copy(
            win_hbm.at[r, t, pl.ds(c * ch, ch)], kv.at[r, t, pl.ds(c * ch, ch)], kv_sem.at[r, t, c]
        )

    def live_of(r):
        return jnp.minimum(lens[r] - SINKS + 1, length)

    def fetch(t):
        def step(r, carry):
            live = live_of(r)
            for c in range(chunks):

                @pl.when(c * ch < live)
                def _():
                    kv_copy(r, t, c).start()

            return carry

        lax.fori_loop(0, rows, step, 0)

    for copy in small:
        copy.start()
    for c in range(3):
        for i in range(halves):
            w_copy(c, i).start()
    small[0].wait()
    fetch(0)
    fetch(1)
    ow_copy = pltpu.make_async_copy(ow_hbm, ow_buf, ow_sem)
    ow_copy.start()
    for copy in small[1:]:
        copy.wait()

    routing_tables(groups, heads_axis, idx, rw, big_out, meta_out)

    place = jnp.concatenate([jnp.full((1, HD // 2), lens[r], jnp.int32) for r in range(rows)], axis=0)
    angles = place.astype(F32) * freq[...]
    cosine, sine = jnp.cos(angles), jnp.sin(angles)
    cos = jnp.concatenate([cosine, cosine], axis=1)
    sin = jnp.concatenate([-sine, sine], axis=1)

    x = hidden[...].astype(F32)
    ms = jnp.mean(x * x, axis=-1, keepdims=True)
    normed = (x * lax.rsqrt(ms + EPSILON) * gain[...]).astype(BF)
    proj = []
    for c in range(3):
        total_c = bias[c : c + 1, :]
        for i in range(halves):
            w_copy(c, i).wait()
            total_c = total_c + dot(
                normed[:, i * wc : (i + 1) * wc], w_buf[c, i * wc : (i + 1) * wc, :]
            )
        proj.append(total_c)

    def rotate(v):
        outs = []
        for h in range(local // HD):
            part_h = v[:, h * HD : (h + 1) * HD]
            outs.append(part_h * cos + pltpu.roll(part_h, HD // 2, 1) * sin)
        return jnp.concatenate(outs, axis=1)

    q = rotate(proj[0]).astype(BF).astype(F32)
    kf = rotate(proj[1]).astype(BF)
    vf = proj[2].astype(BF)
    new_kv[...] = jnp.stack([kf.astype(F32), vf.astype(F32)], axis=1).astype(BF)
    head_mask = iota((ROWS, local), 1) // HD == iota((ROWS, local), 0)
    q3 = jnp.where(head_mask[None], q[:, None, :], 0.0)
    qbd[...] = q3.astype(BF)
    fresh_scores = jnp.sum(q3 * kf.astype(F32)[:, None, :], axis=-1, keepdims=True)

    sink_s = [
        lax.dot_general(qbd[r], sink[r, 0], NT, preferred_element_type=F32) / math.sqrt(HD)
        for r in range(rows)
    ]

    def score_step(r, carry):
        used = (live_of(r) + ch - 1) // ch
        for n in range(1, chunks + 1):

            @pl.when(used == n)
            def _():
                for c in range(n):
                    kv_copy(r, 0, c).wait()
                sc[r, :, : n * ch] = lax.dot_general(
                    qbd[r], kv[r, 0, : n * ch, :], NT, preferred_element_type=F32
                )

        return carry

    lax.fori_loop(0, rows, score_step, 0)

    pos = iota((ROWS, length), 1)
    rest = []
    vf32 = vf.astype(F32)
    for r in range(rows):
        slot = lax.rem(lens[r] - SINKS, length)
        is_fresh = pos == slot
        s = jnp.where(is_fresh, fresh_scores[r], sc[r]) / math.sqrt(HD)
        s = jnp.where(pos < live_of(r), s, -jnp.inf)
        ss = sink_s[r]
        top = jnp.maximum(
            jnp.max(s, axis=-1, keepdims=True), jnp.max(ss, axis=-1, keepdims=True)
        )
        e = jnp.exp(s - top)
        es = jnp.exp(ss - top)
        tot = jnp.sum(e, axis=-1, keepdims=True) + jnp.sum(es, axis=-1, keepdims=True)
        w = (e / tot).astype(BF).astype(F32)
        fresh_w = jnp.sum(jnp.where(is_fresh, w, 0.0), axis=-1, keepdims=True)
        rest.append(fresh_w * vf32[r : r + 1, :] + dot((es / tot).astype(BF), sink[r, 1]))
        wts[r] = jnp.where(is_fresh, 0.0, w).astype(BF)

    def value_step(r, carry):
        used = (live_of(r) + ch - 1) // ch
        for n in range(1, chunks + 1):

            @pl.when(used == n)
            def _():
                for c in range(n):
                    kv_copy(r, 1, c).wait()
                acc[r] = dot(wts[r, :, : n * ch], kv[r, 1, : n * ch, :])

        return carry

    lax.fori_loop(0, rows, value_step, 0)

    attended = [
        jnp.sum(jnp.where(head_mask, acc[r] + rest[r], 0.0), axis=0, keepdims=True)
        for r in range(rows)
    ]
    attended = jnp.concatenate(attended, axis=0).astype(BF)
    ow_copy.wait()
    mine = dot(attended, ow_buf[...])
    part[...] = mine
    part_low[...] = mine.astype(BF)


def attend(groups, heads_axis, freq, lens, hidden, gain, bias, sink, idx, rw, w, win, ow):
    rows, width = hidden.shape
    local = bias.shape[1]
    length = win.shape[2]
    chunks = 4 if length % 4 == 0 else 1
    span = rows + CAP * groups
    return pl.pallas_call(
        functools.partial(attend_kernel, groups, heads_axis),
        out_shape=(
            jax.ShapeDtypeStruct((rows, width), F32),
            jax.ShapeDtypeStruct((rows, width), BF),
            jax.ShapeDtypeStruct((rows, 2, local), BF),
            jax.ShapeDtypeStruct((groups * span, groups * rows), BF),
            jax.ShapeDtypeStruct((groups * rows, width // groups), BF),
        ),
        in_specs=[VM] + [HB] * 10,
        out_specs=(VM,) * 5,
        scratch_shapes=[
            pltpu.SMEM(lens.shape, lens.dtype),
            pltpu.VMEM(hidden.shape, hidden.dtype),
            pltpu.VMEM(gain.shape, gain.dtype),
            pltpu.VMEM(bias.shape, bias.dtype),
            pltpu.VMEM(sink.shape, sink.dtype),
            pltpu.VMEM(idx.shape, idx.dtype),
            pltpu.VMEM(rw.shape, rw.dtype),
            pltpu.VMEM((3, width, local), BF),
            pltpu.VMEM((rows, 2, length, local), BF),
            pltpu.VMEM((local, width), BF),
            pltpu.VMEM((rows, ROWS, local), BF),
            pltpu.VMEM((rows, ROWS, length), F32),
            pltpu.VMEM((rows, ROWS, length), BF),
            pltpu.VMEM((rows, ROWS, local), F32),
            pltpu.SemaphoreType.DMA((7,)),
            pltpu.SemaphoreType.DMA((3, 2)),
            pltpu.SemaphoreType.DMA((rows, 2, chunks)),
            pltpu.SemaphoreType.DMA(()),
        ],
        compiler_params=params(52 * MB),
        name="attend",
    )(freq, *map(stay, (lens, hidden, gain, bias, sink, idx, rw, w, win, ow)))


def dispatch_kernel(groups, others, mine, hidden, gain, gate_vec, big, meta, *rest):
    parts, (send, own_out, keep) = rest[:others], rest[others:]
    rows, width = hidden.shape
    summed = mine[...]
    for p in parts:
        summed = summed + p[...].astype(F32)
    resid = hidden[...].astype(F32) + summed
    keep[...] = resid
    ms = jnp.mean(resid * resid, axis=-1, keepdims=True)
    tokens = (resid * lax.rsqrt(ms + EPSILON) * gain[...]).astype(BF).astype(F32)
    gate = jax.nn.sigmoid(jnp.sum(tokens * gate_vec[...], axis=-1, keepdims=True))
    w = width // groups
    stacked = jnp.concatenate([tokens[:, j * w : (j + 1) * w] for j in range(groups)], axis=0)
    placed = dot(big[...], stacked.astype(BF)).astype(BF)
    lane = iota((rows, w), 1)
    extra = jnp.zeros((rows, w), F32)
    for p, term in enumerate(split3(gate)):
        extra = extra + jnp.where(lane == 3 * CAP + p, term, 0.0)
    span = placed.shape[0] // groups
    full = send.shape[0] // groups
    for g in range(groups):
        send[g * full : g * full + span, :] = placed[g * span : (g + 1) * span, :]
        told = meta[g * rows : (g + 1) * rows, :].astype(F32) + extra
        send[g * full + span : (g + 1) * full, :] = told.astype(BF)
    slot = own_out.shape[1]
    start = pl.multiple_of(lax.axis_index("head") * slot, HD)
    own_out[...] = keep[:, pl.ds(start, slot)]


def dispatch(groups, slot, mine, parts, hidden, gain, gate_vec, big, meta):
    rows, width = hidden.shape
    return pl.pallas_call(
        functools.partial(dispatch_kernel, groups, len(parts)),
        out_shape=(
            jax.ShapeDtypeStruct((big.shape[0] + groups * rows, width // groups), BF),
            jax.ShapeDtypeStruct((rows, slot), F32),
        ),
        in_specs=[VM] * (6 + len(parts)),
        out_specs=(VM,) * 2,
        scratch_shapes=[pltpu.VMEM((rows, width), F32)],
        compiler_params=params(16 * MB),
        name="dispatch",
    )(mine, hidden, gain, gate_vec, big, meta, *parts)


def shared_in_kernel(groups, rows, arrived, weights, out, buf, sem):
    span = arrived.shape[0] // groups
    x = jnp.concatenate(
        [arrived[g * span : g * span + rows, :] for g in range(groups)], axis=0
    )
    tokens = x.shape[0]
    copies = []
    for i, first in enumerate(range(0, weights.shape[2], SPAN)):
        at = slice(first, min(first + SPAN, weights.shape[2]))
        both = jnp.concatenate([dot(x, weights[0, :, at]), dot(x, weights[1, :, at])], axis=0)
        buf[at, :] = both.T.astype(BF)
        copies.append(pltpu.make_async_copy(buf.at[at], out.at[at], sem.at[i]))
        copies[-1].start()
    for copy in copies:
        copy.wait()


def shared_in(groups, rows, arrived, weights):
    shape = (weights.shape[2], 2 * groups * rows)
    return pl.pallas_call(
        functools.partial(shared_in_kernel, groups, rows),
        out_shape=jax.ShapeDtypeStruct(shape, BF),
        in_specs=[VM] * 2,
        out_specs=HB,
        scratch_shapes=[
            pltpu.VMEM(shape, BF),
            pltpu.SemaphoreType.DMA((pl.cdiv(shape[0], SPAN),)),
        ],
        compiler_params=params(16 * MB),
        name="shared_in",
    )(arrived, weights)


def expert_kernel(groups, rows, arrived, gu_hbm, down_hbm, out, gu, down, gu_sem, down_sem):
    pieces = down_sem.shape[0]
    piece = down.shape[0] // pieces

    def gu_copy(t, i):
        at = pl.ds(i * piece, piece)
        return pltpu.make_async_copy(gu_hbm.at[t, at], gu.at[t, at], gu_sem.at[t, i])

    def down_copy(i):
        at = pl.ds(i * piece, piece)
        return pltpu.make_async_copy(down_hbm.at[at], down.at[at], down_sem.at[i])

    for i in range(pieces):
        gu_copy(0, i).start()
        gu_copy(1, i).start()
    for i in range(pieces):
        down_copy(i).start()

    slots = groups * CAP
    total = arrived.shape[0]
    span = total // groups
    line, lane = iota((groups * slots, total), 0), iota((groups * slots, total), 1)
    j, g, c = line // slots, line % slots // CAP, line % CAP
    pickm = one(lane == g * span + rows + j * CAP + c).astype(BF)
    x = dot(pickm, arrived[...])
    x = jnp.concatenate(
        [x[jj * slots : (jj + 1) * slots, :] for jj in range(groups)], axis=1
    ).astype(BF)
    hidden = []
    for i in range(pieces):
        at = slice(i * piece, (i + 1) * piece)
        gu_copy(0, i).wait()
        gate = lax.dot_general(x, gu[0, at, :], NT, preferred_element_type=F32)
        gu_copy(1, i).wait()
        up = lax.dot_general(x, gu[1, at, :], NT, preferred_element_type=F32)
        hidden.append((jax.nn.silu(gate) * up).astype(BF))
    result = jnp.zeros((slots, down.shape[1]), F32)
    for i in range(pieces):
        down_copy(i).wait()
        result = result + dot(hidden[i], down[i * piece : (i + 1) * piece, :])
    out[...] = result


def experts(groups, rows, arrived, gate_up, down):
    fe, width = down.shape
    pieces = fe // 352 if fe % 352 == 0 else 1
    slots = groups * CAP
    return pl.pallas_call(
        functools.partial(expert_kernel, groups, rows),
        out_shape=jax.ShapeDtypeStruct((slots, width), F32),
        in_specs=[VM, HB, HB],
        out_specs=VM,
        scratch_shapes=[
            pltpu.VMEM(gate_up.shape, BF),
            pltpu.VMEM(down.shape, BF),
            pltpu.SemaphoreType.DMA((2, pieces)),
            pltpu.SemaphoreType.DMA((pieces,)),
        ],
        compiler_params=params(32 * MB),
        cost_estimate=pl.CostEstimate(
            flops=6 * slots * fe * width, transcendentals=slots * fe, bytes_accessed=6 * fe * width
        ),
        name="experts",
    )(arrived, stay(gate_up), stay(down))


def give_back_kernel(groups, heads_axis, rows, sums, down, routed, arrived, out):
    total = sums[0].astype(F32)
    for g in range(1, groups):
        total = total + sums[g].astype(F32)
    tokens = groups * rows
    hidden = jax.nn.silu(total) * pltpu.roll(total, tokens, 1)
    hidden = hidden[:, :tokens].T.astype(BF)
    span = arrived.shape[0] // groups
    told = jnp.concatenate(
        [arrived[(g + 1) * span - rows : (g + 1) * span, :HD] for g in range(groups)], axis=0
    ).astype(F32)

    def column(k):
        return told[:, 3 * k : 3 * k + 1] + told[:, 3 * k + 1 : 3 * k + 2] + told[:, 3 * k + 2 : 3 * k + 3]

    gate = column(CAP)
    weight = [column(c) for c in range(CAP)]
    w = down.shape[2]
    ratio = groups // heads_axis
    for j in range(groups):
        shared = gate * dot(hidden, down[j])
        h, half = j // ratio, j % ratio
        for g in range(groups):
            at = slice(g * rows, (g + 1) * rows)
            value = shared[at]
            for c in range(CAP):
                line = routed[g * CAP + c : g * CAP + c + 1, j * w : (j + 1) * w]
                value = value + weight[c][at] * line
            to = (g * heads_axis + h) * rows
            out[to : to + rows, half * w : (half + 1) * w] = value.astype(BF)


def give_back(groups, heads_axis, rows, sums, down, routed, arrived):
    return pl.pallas_call(
        functools.partial(give_back_kernel, groups, heads_axis, rows),
        out_shape=jax.ShapeDtypeStruct(
            (groups * heads_axis * rows, routed.shape[1] // heads_axis), BF
        ),
        in_specs=[VM] * 4,
        out_specs=VM,
        compiler_params=params(16 * MB),
        name="give_back",
    )(sums, down, routed, arrived)


def finish_kernel(returned, own, out):
    rows = own.shape[0]
    total = own[...]
    for i in range(returned.shape[0] // rows):
        total = total + returned[i * rows : (i + 1) * rows, :].astype(F32)
    out[...] = total.astype(BF)


def finish(returned, own):
    return pl.pallas_call(
        finish_kernel,
        out_shape=jax.ShapeDtypeStruct(own.shape, BF),
        in_specs=[VM] * 2,
        out_specs=VM,
        compiler_params=params(16 * MB),
        name="finish",
    )(returned, own)


def local(
    hidden_state,
    attend_gain,
    input_weight,
    input_bias,
    output_weight,
    window_cache,
    sink_cache,
    lengths,
    expert_index,
    router_weight,
    mixture_gain,
    expert_gate_up,
    expert_down,
    shared_gate_up,
    shared_down,
    shared_gate,
):
    rows, width = hidden_state.shape
    local_width = input_weight.shape[2]
    groups = lax.axis_size("req")
    heads_axis = lax.axis_size("head")
    slot = width // heads_axis
    half = HD // 2
    frequencies = F32(ROPE_BASE) ** (-(2.0 / HD) * jnp.arange(half).astype(F32))
    down = shared_down.reshape(groups, shared_down.shape[0] // groups, shared_down.shape[1])
    down = lax.all_to_all(down, "req", split_axis=0, concat_axis=0, tiled=True)

    part, low, new_kv, big, meta = attend(
        groups,
        heads_axis,
        frequencies[None],
        lengths,
        hidden_state,
        attend_gain[None],
        input_bias,
        sink_cache,
        expert_index.T,
        router_weight.T,
        jnp.transpose(input_weight, (1, 0, 2)),
        window_cache,
        output_weight,
    )
    parts = [
        lax.ppermute(part if k == 1 else low, "head", [(j, j ^ k) for j in range(heads_axis)])
        for k in reversed(range(1, heads_axis))
    ]
    parts, down = lax.optimization_barrier((parts, down))
    send, own = dispatch(
        groups, slot, part, parts, hidden_state, mixture_gain[None], shared_gate[None], big, meta
    )
    arrived = lax.all_to_all(send, "req", split_axis=0, concat_axis=0, tiled=True)
    sums = shared_in(groups, rows, arrived, shared_gate_up)
    sums = sums.reshape(groups, sums.shape[0] // groups, sums.shape[1])
    sums = lax.all_to_all(sums, "req", split_axis=0, concat_axis=0, tiled=True)
    routed = experts(groups, rows, arrived, expert_gate_up, expert_down)
    back = give_back(groups, heads_axis, rows, sums, down, routed, arrived)
    returned = lax.all_to_all(back, ("req", "head"), split_axis=0, concat_axis=0, tiled=True)
    return finish(returned, own), new_kv


def solution(mesh):
    return jax.shard_map(
        local,
        mesh=mesh,
        in_specs=(
            P("req", None),
            P(),
            P(None, None, "head"),
            P(None, "head"),
            P("head", None),
            P("req", None, None, "head"),
            P("req", None, None, "head"),
            P("req"),
            P("req", None),
            P("req", None),
            P(),
            P(None, ("req", "head"), None),
            P(("req", "head"), None),
            P(None, "req", "head"),
            P("head", "req"),
            P(),
        ),
        out_specs=(P("req", "head"), P("req", None, "head")),
        check_vma=False,
    )
```
